32 devices in a mesh: lat: 4 (over y, core), lon: 8 (over z, x).
Axes of the slice: x: 2, y: 2, z: 4, core: 2. Of those that a mesh axis runs over, the one named last changes fastest.
Arguments:
- field_in: bfloat16 [512, 64, 300], P('lat', 'lon'), may hold values from -6 to 6
- sea_mask: int32 [512, 64], P('lat', 'lon'), may hold values 0 or 1
- mirror: int32 [64], replicated, may hold values from 0 to 63, as said below
- kernel: float32 [49, 300], replicated, may hold values from -0.875 to 0.875
- norm_gain: float32 [300], replicated, may hold values from 0.1 to 1.9
- proj_in: bfloat16 [300, 1200], replicated, may hold values from -0.375 to 0.375
- proj_out: bfloat16 [1200, 300], replicated, may hold values from -0.1875 to 0.1875
- cotangent: bfloat16 [512, 64, 300], P('lat', 'lon'), may hold values from -6 to 6
Outputs:
- block_out: bfloat16 [512, 64, 300], P('lat', 'lon')
- grad_field: bfloat16 [512, 64, 300], P('lat', 'lon')
- grad_in: float32 [300, 1200], replicated
- grad_out: float32 [1200, 300], replicated
- grad_kernel: float32 [49, 300], replicated
- grad_gain: float32 [300], replicated
The draws below stay inside these ranges and needn't reach their ends.
Inputs may be any that keep to these rules, and one draw needn't show every extreme that they name: mirror[i] = (s - 1 - i) mod 64 for one s, so mirror[mirror[i]] = i.
All inputs are finite; a program needn't handle non-finite values. No bound on the sum of `sea_mask` on one device may be relied on, other than what follows from the above.
Results may differ from the reference program's by a relative error of at most 0.0057.
Values may be sent and summed in bfloat16 or wider, within the bound.
No kernel may reach another device: no remote copies, remote signals or barrier semaphores. Data moves between devices by JAX's collectives and lax.ppermute only.
A program may use at most 128 MiB of HBM per device.

```python
import jax
import jax.numpy as jnp
from jax import lax

C = 300
H = 1200
NLAT = 512
NLON = 64


def draw_mirror(key, part):
    pivot = jax.random.randint(key, (), 0, NLON)
    column = jnp.arange(NLON, dtype=jnp.int32)
    return ((pivot - 1 - column) % NLON).astype(jnp.int32)


def place_ends(entries, stream_key, smallest, largest):
    spot = [jax.random.randint(jax.random.fold_in(stream_key, axis), (), 0, length) for axis, length in enumerate(entries.shape)]
    main_axis = entries.shape.index(max(entries.shape))
    beside = spot[:main_axis] + [(spot[main_axis] + 1) % entries.shape[main_axis]] + spot[main_axis + 1:]
    return entries.at[tuple(spot)].set(smallest).at[tuple(beside)].set(largest)


def block_levels(stream_key, extent, split, low, top_value):
    level, own = 1.0, jax.random.fold_in(stream_key, 6)
    for dim, shards_of in split:
        heights = jnp.exp(jax.random.uniform(jax.random.fold_in(own, dim), (shards_of,), jnp.float32, low / len(split), top_value / len(split)))
        level = level * jnp.repeat(heights, extent[dim] // shards_of).reshape([-1 if axis == dim else 1 for axis in range(len(extent))])
    return level


def gaussian(stream_key, extent, spread, bound, pieces=(), kind=jnp.bfloat16):
    factor_of = block_levels(stream_key, extent, pieces, -0.22, 0.18) if pieces else 1.0
    values = jax.random.normal(stream_key, extent, jnp.float32) * spread * factor_of
    return jnp.minimum(jnp.maximum(values, -bound), bound).astype(kind)


def setup_inputs(seed: int = 0) -> dict:
    seeds = jax.random.split(jax.random.key(seed), 9)
    return {
        "field_in": gaussian(seeds[0], (NLAT, NLON, C), 1.0, 6.0, ((0, 4), (1, 8))),
        "sea_mask": place_ends((jax.random.randint(seeds[1], (NLAT, NLON), 0, 4) < 3).astype(jnp.int32), jax.random.fold_in(seeds[1], 1), 0, 1),
        "mirror": draw_mirror(jax.random.fold_in(seeds[8], 71), 0),
        "kernel": gaussian(seeds[3], (49, C), 49 ** -0.5, 0.875, (), jnp.float32),
        "norm_gain": jnp.clip(1.0 + 0.18 * jax.random.normal(seeds[4], (C,), jnp.float32), 0.1, 1.9),
        "proj_in": gaussian(seeds[5], (C, H), C ** -0.5, 0.375),
        "proj_out": gaussian(seeds[6], (H, C), H ** -0.5, 0.1875),
        "cotangent": gaussian(seeds[7], (NLAT, NLON, C), 1.0, 6.0, ((0, 4), (1, 8))),
    }


def gelu_pair(value):
    coeff = 0.7978845608028654
    inner = coeff * (value + 0.044715 * value * value * value)
    tanh_val = jnp.tanh(inner)
    result = 0.5 * value * (1.0 + tanh_val)
    slope = 0.5 * (1.0 + tanh_val) + 0.5 * value * (1.0 - tanh_val * tanh_val) * coeff * (1.0 + 0.134145 * value * value)
    return (result, slope)

def depthwise(ext, kernel, nrows, ncols):
    total = jnp.zeros((nrows, ncols, kernel.shape[1]), jnp.float32)
    for tap_a in range(7):
        for tap_b in range(7):
            total = total + kernel[7 * tap_a + tap_b] * ext[tap_a:tap_a + nrows, tap_b:tap_b + ncols].astype(jnp.float32)
    return total

def local_block(conv_flat, field_flat, mask_col, cot_flat, norm_gain, proj_in, proj_out):
    mean = lax.optimization_barrier(jnp.mean(conv_flat, axis=-1, keepdims=True))
    centered = conv_flat - mean
    var = lax.optimization_barrier(jnp.mean(centered * centered, axis=-1, keepdims=True))
    rstd = lax.rsqrt(var + 1e-06)
    nhat = centered * rstd
    normed = (nhat * norm_gain).astype(jnp.bfloat16)
    pre = jnp.dot(normed, proj_in, preferred_element_type=jnp.float32)
    act, slope = gelu_pair(pre)
    act = act.astype(jnp.bfloat16)
    mixed = jnp.dot(act, proj_out, preferred_element_type=jnp.float32)
    result = (mask_col * (field_flat + mixed)).astype(jnp.bfloat16)
    back = cot_flat * mask_col
    dw_out = lax.dot_general(act, back, (((0,), (0,)), ((), ())), preferred_element_type=jnp.float32)
    grad_hidden = lax.dot_general(back, proj_out, (((1,), (1,)), ((), ())), preferred_element_type=jnp.float32)
    grad_pre = (grad_hidden * slope).astype(jnp.bfloat16)
    dw_in = lax.dot_general(normed, grad_pre, (((0,), (0,)), ((), ())), preferred_element_type=jnp.float32)
    grad_norm = lax.dot_general(grad_pre, proj_in, (((1,), (1,)), ((), ())), preferred_element_type=jnp.float32)
    dgain = lax.optimization_barrier(jnp.sum(grad_norm * nhat, axis=0))
    scaled = grad_norm * norm_gain
    gconv = rstd * (scaled - lax.optimization_barrier(jnp.mean(scaled, axis=-1, keepdims=True)) - nhat * lax.optimization_barrier(jnp.mean(scaled * nhat, axis=-1, keepdims=True)))
    return (result, gconv.astype(jnp.bfloat16), dw_in, dw_out, dgain)

def reference(field_in, sea_mask, mirror, kernel, norm_gain, proj_in, proj_out, cotangent):
    maskf = sea_mask.astype(jnp.bfloat16)[:, :, None]
    masked = field_in * maskf
    wrapped = jnp.concatenate([masked[:, NLON - 3:], masked, masked[:, :3]], axis=1)
    ext_cols = ((jnp.arange(NLON + 6, dtype=jnp.int32) - 3) % NLON).astype(jnp.int32)
    fold_cols = jnp.take(mirror, ext_cols)
    north = jnp.take(masked[NLAT - 3:][::-1], fold_cols, axis=1)
    south = jnp.zeros((3, NLON + 6, C), field_in.dtype)
    ext = jnp.concatenate([south, wrapped, north], axis=0)
    conv = depthwise(ext, kernel, NLAT, NLON)

    def row_step(carry, items):
        conv_row, field_row, mask_row, cot_row = items
        out_row, gconv_row, dw_in, dw_out, dgain = local_block(conv_row, field_row, mask_row, cot_row, norm_gain, proj_in, proj_out)
        return ((carry[0] + dw_in, carry[1] + dw_out, carry[2] + dgain), (out_row, gconv_row))
    init = (jnp.zeros((C, H), jnp.float32), jnp.zeros((H, C), jnp.float32), jnp.zeros((C,), jnp.float32))
    sums, rows_out = lax.scan(row_step, init, (conv, field_in, maskf, cotangent))
    dw_in, dw_out, dgain = sums
    block_out, gconv = rows_out
    gconv_f = gconv.astype(jnp.float32)
    taps = []
    for tap_a in range(7):
        for tap_b in range(7):
            taps.append(lax.optimization_barrier(jnp.sum(gconv_f * ext[tap_a:tap_a + NLAT, tap_b:tap_b + NLON].astype(jnp.float32), axis=(0, 1))))
    dkernel = jnp.stack(taps, axis=0)
    dext = jnp.zeros((NLAT + 6, NLON + 6, C), jnp.float32)
    for tap_a in range(7):
        for tap_b in range(7):
            dext = dext.at[tap_a:tap_a + NLAT, tap_b:tap_b + NLON].add(kernel[7 * tap_a + tap_b] * gconv_f)
    dwrap = dext[:, 3:NLON + 3]
    dwrap = dwrap.at[:, :3].add(dext[:, NLON + 3:])
    dwrap = dwrap.at[:, NLON - 3:].add(dext[:, :3])
    dmasked = dwrap[3:NLAT + 3]
    fold = jnp.take(dwrap[NLAT + 3:][::-1], mirror, axis=1)
    dmasked = dmasked.at[NLAT - 3:].add(fold)
    back = (cotangent * maskf).astype(jnp.float32)
    grad_field = (back + maskf * dmasked).astype(jnp.bfloat16)
    factor = 1.0 / jnp.sqrt(jnp.float32(NLAT * NLON))
    return (block_out, grad_field, dw_in * factor, dw_out * factor, dkernel * factor, dgain * factor)
```

```python
import jax
import jax.numpy as jnp
import numpy as np
from jax import lax
from jax.experimental import pallas as pl
from jax.experimental.pallas import tpu as pltpu
from jax.sharding import PartitionSpec as P

F32 = jnp.float32
BF16 = jnp.bfloat16
AXES = ("lat", "lon")
SUB = 8
COLS = 8
QC = COLS + 6
LT = 3
CP = LT * 128
HB = 256
VM = pl.BlockSpec(memory_space=pltpu.VMEM)
SM = pl.BlockSpec(memory_space=pltpu.SMEM)
LIMIT = 60 * 1024 * 1024

EVEN_LON, EVEN_LAT, IS_TOP, LON, START, ME = range(6)


def params():
    return pltpu.CompilerParams(vmem_limit_bytes=LIMIT)


def lanes(l, width):
    return min(128, width - 128 * l)


def tap_rows(k_ref, ks, width):
    ks[...] = jnp.zeros_like(ks)
    for l in range(LT):
        w = lanes(l, width)
        ks[l, : k_ref.shape[0], :w] = k_ref[:, 128 * l : 128 * l + w]


def prepare_kernel(sc, mask_ref, f_ref, c_ref, mf_ref, bk_ref, mk_ref, p1_ref, p2_ref, pad, rows, ct):
    nrows, _, width = f_ref.shape
    tt = nrows // SUB
    m_t = mask_ref[...].astype(F32).T
    for src, dst in ((f_ref, mf_ref), (c_ref, ct)):
        pad[:, :, 256:] = jnp.zeros((nrows, COLS, 128), BF16)
        pad[:, :, :width] = src[...]
        for j in range(nrows):
            s, t = j // tt, j % tt
            m = jnp.broadcast_to(m_t[:, j : j + 1], (COLS, 128))
            at = pl.ds(t * 64 + s, COLS, stride=SUB)
            if src is f_ref:
                mk_ref[at, :] = m
            for l in range(LT):
                v = pad[j, :, 128 * l : 128 * (l + 1)].astype(F32) * m
                dst[l, at, :] = v
                if src is f_ref and (j < 3 or j >= nrows - 3):
                    rows[(0 if j < 3 else 3) + (j if j < 3 else j - nrows + 3), :, 128 * l : 128 * (l + 1)] = v
    for l in range(LT):
        bk_ref[:, 128 * l : 128 * (l + 1)] = ct[l].astype(BF16)
    even = sc[EVEN_LAT]
    p1_ref[...] = rows[pl.ds(3 * even, 3)].astype(BF16)
    p2_ref[...] = rows[pl.ds(3 - 3 * even, 3)].astype(BF16)


def strips_kernel(sc, x_ref, p1_ref, p2_ref, q1_ref, q2_ref, lu):
    n = x_ref.shape[1]
    tt = n // 64
    even_lat, even_lon = sc[EVEN_LAT], sc[EVEN_LON]
    lower = jnp.where(even_lat == 1, p2_ref[...].astype(F32), p1_ref[...].astype(F32))
    upper = jnp.where(even_lat == 1, p1_ref[...].astype(F32), p2_ref[...].astype(F32))
    for l in range(LT):
        for r in range(3):
            lu[l, 8 * r : 8 * r + 8, :] = lower[r, :, 128 * l : 128 * (l + 1)]
            lu[l, 24 + 8 * r : 32 + 8 * r, :] = upper[r, :, 128 * l : 128 * (l + 1)]
        lu[l, 48:, :] = jnp.zeros((16, 128), F32)
    for q_ref, first in ((q1_ref, 5 * even_lon), (q2_ref, 5 - 5 * even_lon)):
        for l in range(LT):
            for c in range(3):
                for t in range(0, tt, 2):
                    a = x_ref[l, pl.ds(pl.multiple_of(t * 64 + (first + c) * 8, 8), 8), :]
                    b = x_ref[l, pl.ds(pl.multiple_of(t * 64 + 64 + (first + c) * 8, 8), 8), :]
                    q_ref[l, (c * tt + t) * 8 : (c * tt + t) * 8 + 16, :] = jnp.concatenate([a, b], 0).astype(BF16)
            k = [lu[l, pl.ds(first + c, 8, stride=8), :] for c in range(3)]
            k.append(jnp.zeros((8, 128), F32))
            q_ref[l, 3 * tt * 8 : 3 * tt * 8 + 32, :] = jnp.concatenate(k, 0).astype(BF16)


def extend(sc, ext, x_ref, q1_ref, q2_ref, p1_ref, p2_ref):
    tt = x_ref.shape[1] // 64
    even_lat, even_lon, top = sc[EVEN_LAT], sc[EVEN_LON], sc[IS_TOP]
    for l in range(LT):
        for t in range(tt):
            ext[l, ((t + 3) * QC + 3) * 8 : ((t + 3) * QC + 3) * 8 + 64, :] = x_ref[l, t * 64 : t * 64 + 64, :]
    sides = ((q1_ref, 11 * even_lon), (q2_ref, 11 - 11 * even_lon))
    for q_ref, first in sides:
        for l in range(LT):
            for c in range(3):
                for t in range(0, tt, 2):
                    v = q_ref[l, (c * tt + t) * 8 : (c * tt + t) * 8 + 16, :].astype(F32)
                    for u in range(2):
                        ext[l, pl.ds(pl.multiple_of(((t + u + 3) * QC + first + c) * 8, 8), 8), :] = v[8 * u : 8 * u + 8]
    for l in range(LT):
        for r in range(3):
            for q in range(QC):
                lo = ext[l, ((tt + r) * QC + q) * 8 : ((tt + r) * QC + q) * 8 + 8, :]
                ext[l, (r * QC + q) * 8 : (r * QC + q) * 8 + 8, :] = pltpu.roll(lo, 1, 0)
                hi = ext[l, ((3 + r) * QC + q) * 8 : ((3 + r) * QC + q) * 8 + 8, :]
                at = ((tt + 3 + r) * QC + q) * 8
                ext[l, at : at + 8, :] = pltpu.roll(hi, 7, 0)
    keep = (1 - top).astype(F32)
    p1, p2 = p1_ref[...].astype(F32), p2_ref[...].astype(F32)
    lower = jnp.where(even_lat == 1, p2, p1)
    upper = jnp.where(even_lat == 1, p1, p2) * keep
    for l in range(LT):
        for r in range(3):
            ext[l, pl.ds((r * QC + 3) * 8, 8, stride=8), :] = lower[r, :, 128 * l : 128 * (l + 1)]
            ext[l, pl.ds(((tt + 3 + r) * QC + 3) * 8 + 7, 8, stride=8), :] = upper[r, :, 128 * l : 128 * (l + 1)]
    for q_ref, first in sides:
        for l in range(LT):
            corner = q_ref[l, 3 * tt * 8 : 3 * tt * 8 + 32, :].astype(F32)
            for c in range(3):
                for r in range(3):
                    ext[l, pl.ds((r * QC + first + c) * 8, 1), :] = corner[8 * c + r : 8 * c + r + 1]
                    ext[l, pl.ds(((tt + 3 + r) * QC + first + c) * 8 + 7, 1), :] = corner[8 * c + 3 + r : 8 * c + 4 + r] * keep


def fold_rows(sc, mir, fold_ref, buf, dst, base):
    units = fold_ref.shape[0]
    for l in range(LT):
        for u in range(units):
            for r in range(3):
                at = (u * 3 + r) * 8
                buf[l, at : at + 8, :] = fold_ref[u, r, :, 128 * l : 128 * (l + 1)].astype(F32)
    total = mir.shape[0]
    for q in range(QC):
        col = sc[START] - 3 + q
        col = jnp.where(col < 0, col + total, col)
        col = jnp.where(col >= total, col - total, col)
        m = mir[col]
        unit = lax.bitwise_xor(lax.shift_right_logical(m, 3), sc[LON])
        at = unit * 24 + lax.bitwise_and(m, 7)
        for k in range(3):
            for l in range(LT):
                dst[l, pl.ds(base + (k * QC + q) * 8 + 7, 1), :] = buf[l, pl.ds(at + (2 - k) * 8, 1), :]


def correlate(ext, ks, tt, flip, store):
    for l in range(LT):

        def column(i, carry, l=l):
            acc = [None] * tt
            for b in range(7):
                k = []
                for a in range(7):
                    tap = 7 * a + b
                    tap = 48 - tap if flip else tap
                    k.append(jnp.broadcast_to(ks[l, tap : tap + 1, :], (8, 128)))
                for u in range(tt + 6):
                    e = ext[l, pl.ds(pl.multiple_of((u * QC + i + b) * 8, 8), 8), :]
                    for a in range(7):
                        t = u - a
                        if 0 <= t < tt:
                            v = k[a] * e
                            acc[t] = v if acc[t] is None else acc[t] + v
            for t in range(tt):
                store(l, t, i, acc[t])
            return carry

        lax.fori_loop(0, COLS, column, 0)


def block_kernel(
    width, sc, mir, k_ref, gain_ref, win_ref, wout_ref, mf_ref, bk_ref, mk_ref, q1_ref, q2_ref, p1_ref, p2_ref, fold_ref,
    out_ref, ext, gc_ref, g1_ref, g2_ref, dw_ref, dgain_ref,
    ks, buf, conv, normed, act, gp, res, rows,
):
    cells = mf_ref.shape[1]
    tt = cells // 64
    hidden = win_ref.shape[1]
    extend(sc, ext, mf_ref, q1_ref, q2_ref, p1_ref, p2_ref)

    @pl.when(sc[IS_TOP] == 1)
    def _():
        fold_rows(sc, mir, fold_ref, buf, ext, (tt + 3) * QC * 8)

    tap_rows(k_ref, ks, width)

    def put(l, t, i, v):
        conv[pl.ds(pl.multiple_of(t * 64 + i * 8, 8), 8), 128 * l : 128 * (l + 1)] = v

    correlate(ext, ks, tt, False, put)
    size = 256
    gain = gain_ref[...]
    valid = (lax.broadcasted_iota(jnp.int32, (1, CP), 1) < width).astype(F32)
    dgain_ref[...] = jnp.zeros_like(dgain_ref)
    inv = 1.0 / width
    coeff = 0.7978845608028654

    def chunk(n, carry):
        at = pl.ds(pl.multiple_of(n * size, size), size)
        x = conv[at, :]
        mean = jnp.sum(x, axis=-1, keepdims=True) * inv
        cen = (x - mean) * valid
        var = jnp.sum(cen * cen, axis=-1, keepdims=True) * inv
        rstd = lax.rsqrt(var + 1e-06)
        nhat = cen * rstd
        nb = (nhat * gain).astype(BF16)
        normed[at, :] = nb
        back = bk_ref[at, :]
        for h in range(0, hidden, HB):
            v = jnp.dot(nb, win_ref[:, h : h + HB], preferred_element_type=F32)
            g = lax.dot_general(back, wout_ref[h : h + HB, :], (((1,), (1,)), ((), ())), preferred_element_type=F32)
            v2 = v * v
            half = 0.5 + 0.5 * jnp.tanh(v * (coeff + (coeff * 0.044715) * v2))
            a = v * half
            slope = half + a * (1.0 - half) * (2.0 * coeff + (2.0 * coeff * 0.134145) * v2)
            act[at, h : h + HB] = a.astype(BF16)
            gp[at, h : h + HB] = (g * slope).astype(BF16)
        mixed = jnp.dot(act[at, :], wout_ref[...], preferred_element_type=F32)
        gn = lax.dot_general(gp[at, :], win_ref[...], (((1,), (1,)), ((), ())), preferred_element_type=F32)
        m = mk_ref[at, :]
        for l in range(LT):
            res[l, at, :] = mf_ref[l, at, :] + m * mixed[:, 128 * l : 128 * (l + 1)]
        dgain_ref[...] += jnp.broadcast_to(jnp.sum(gn * nhat, axis=0, keepdims=True), dgain_ref.shape)
        s = gn * gain
        m1 = jnp.sum(s, axis=-1, keepdims=True) * inv
        m2 = jnp.sum(s * nhat, axis=-1, keepdims=True) * inv
        gc = (rstd * (s - m1 - nhat * m2) * valid).astype(BF16).astype(F32)
        for l in range(LT):
            gc_ref[l, at, :] = gc[:, 128 * l : 128 * (l + 1)]
        return carry

    lax.fori_loop(0, cells // size, chunk, 0)
    for l in range(LT):
        for r in range(3):
            rows[r, :, 128 * l : 128 * (l + 1)] = gc_ref[l, pl.ds(r * 64, 8, stride=8), :]
            rows[3 + r, :, 128 * l : 128 * (l + 1)] = gc_ref[l, pl.ds((tt - 3 + r) * 64 + 7, 8, stride=8), :]
    even = sc[EVEN_LAT]
    g1_ref[...] = rows[pl.ds(3 * even, 3)].astype(BF16)
    g2_ref[...] = rows[pl.ds(3 - 3 * even, 3)].astype(BF16)
    for m, (left, right) in enumerate(((normed, gp), (bk_ref, act))):
        tiles = (hidden // 128) * (DWR // 16)
        for h in range(0, hidden, HB):
            d = lax.dot_general(
                left[...], right[:, h : h + HB], (((0,), (0,)), ((), ())), preferred_element_type=F32
            ).astype(BF16)
            for u in range(HB // 128):
                first = m * tiles + (h // 128 + u) * (DWR // 16)
                for r in range(DWR // 16):
                    dw_ref[first + r] = d[16 * r : 16 * r + 16, 128 * u : 128 * u + 128]
    for j in range(tt * SUB):
        s, t = j // tt, j % tt
        for l in range(LT):
            w = lanes(l, width)
            out_ref[j, :, 128 * l : 128 * l + w] = res[l, pl.ds(t * 64 + s, 8, stride=8), :][:, :w].astype(BF16)


DWR = 304
DKR = 64


def taps_kernel(ext, gc_ref, dgain_ref, dk_ref, part, rows):
    tt = gc_ref.shape[1] // 64
    for l in range(LT):

        def tap_column(b, carry, l=l):
            acc = [jnp.zeros((8, 128), F32)] * 7
            for i in range(COLS):
                g = [gc_ref[l, t * 64 + i * 8 : t * 64 + i * 8 + 8, :] for t in range(tt)]
                for u in range(tt + 6):
                    e = ext[l, pl.ds(pl.multiple_of((u * QC + i + b) * 8, 8), 8), :]
                    for a in range(7):
                        t = u - a
                        if 0 <= t < tt:
                            acc[a] = acc[a] + g[t] * e
            for a in range(7):
                part[l, pl.ds(pl.multiple_of((7 * a + b) * 8, 8), 8), :] = acc[a]
            return carry

        lax.fori_loop(0, 7, tap_column, 0)
    rows[...] = jnp.zeros_like(rows)
    for l in range(LT):
        for k in range(49):
            rows[l, k : k + 1, :] = jnp.sum(part[l, 8 * k : 8 * k + 8, :], axis=0, keepdims=True)
        rows[l, 49:50, :] = dgain_ref[0:1, 128 * l : 128 * (l + 1)]
        for r in range(DKR // 16):
            dk_ref[l * (DKR // 16) + r] = rows[l, 16 * r : 16 * r + 16, :].astype(BF16)


def field_kernel(
    width, sc, mir, k_ref, gc_ref, bk_ref, mk_ref, q1_ref, q2_ref, p1_ref, p2_ref, fold_ref, out_ref, ks, buf, ext, ghost, dm
):
    cells = gc_ref.shape[1]
    tt = cells // 64
    extend(sc, ext, gc_ref, q1_ref, q2_ref, p1_ref, p2_ref)
    tap_rows(k_ref, ks, width)

    def put(l, t, i, v):
        dm[l, pl.ds(pl.multiple_of(t * 64 + i * 8, 8), 8), :] = v

    correlate(ext, ks, tt, True, put)

    @pl.when(sc[IS_TOP] == 1)
    def _():
        ghost[...] = jnp.zeros_like(ghost)
        fold_rows(sc, mir, fold_ref, buf, ghost, 0)
        for l in range(LT):

            def column(i, carry, l=l):
                for k in range(3):
                    at = pl.ds(pl.multiple_of((tt - 1 - k) * 64 + i * 8, 8), 8)
                    acc = dm[l, at, :]
                    for r in range(3 - k):
                        for b in range(7):
                            tap = 7 * (4 + k + r) + b
                            e = ghost[l, pl.ds(pl.multiple_of((r * QC + i + b) * 8, 8), 8), :]
                            acc = acc + jnp.broadcast_to(ks[l, tap : tap + 1, :], (8, 128)) * e
                    dm[l, at, :] = acc
                return carry

            lax.fori_loop(0, COLS, column, 0)

    for l in range(LT):
        for n in range(0, cells, 64):
            dm[l, n : n + 64, :] = dm[l, n : n + 64, :] * mk_ref[n : n + 64, :] + bk_ref[
                n : n + 64, 128 * l : 128 * (l + 1)
            ].astype(F32)
    for j in range(tt * SUB):
        s, t = j // tt, j % tt
        for l in range(LT):
            w = lanes(l, width)
            out_ref[j, :, 128 * l : 128 * l + w] = dm[l, pl.ds(t * 64 + s, 8, stride=8), :][:, :w].astype(BF16)


def unpack_kernel(width, hidden, factor, per, sc, x_ref, gin_ref, gout_ref, gk_ref, gg_ref):
    blocks = (hidden + 127) // 128
    blocks += blocks % 2
    tr = DWR // 16

    def tile(n):
        chunk = lax.bitwise_xor(jnp.int32(n // per), sc[ME])
        return x_ref[chunk * per + n % per].astype(F32) * factor

    for cb in range(blocks):
        w = min(128, hidden - 128 * cb)
        if w <= 0:
            continue
        for r in range(tr):
            rows = min(16, width - 16 * r)
            gin_ref[16 * r : 16 * r + rows, 128 * cb : 128 * cb + w] = tile(cb * tr + r)[:rows, :w]
        parts = [tile((blocks + cb) * tr + r) for r in range(tr)] + [jnp.zeros((CP - DWR, 128), F32)]
        full = jnp.concatenate(parts, axis=0).T
        gout_ref[128 * cb : 128 * cb + w, :] = full[:w, :width]
    for l in range(LT):
        w = lanes(l, width)
        base = 2 * blocks * tr + l * (DKR // 16)
        taps = jnp.concatenate([tile(base + r) for r in range(DKR // 16)], axis=0)
        gk_ref[:, 128 * l : 128 * l + w] = taps[:49, :w]
        gg_ref[:, 128 * l : 128 * l + w] = taps[49:50, :w]


def swaps(n_lat, n_lon, bits):
    ml, mo = bits
    return [(l * n_lon + o, (l ^ ml) * n_lon + (o ^ mo)) for l in range(n_lat) for o in range(n_lon)]


def lat_swaps(n_lat, n_lon):
    first = [(l * n_lon + o, (l ^ 1) * n_lon + o) for l in range(n_lat) for o in range(n_lon)]
    second = []
    for l in range(n_lat):
        for o in range(n_lon):
            if l == n_lat - 1:
                second.append((l * n_lon + o, l * n_lon + (o ^ 1)))
            elif l > 0:
                other = l + 1 if l % 2 else l - 1
                second.append((l * n_lon + o, other * n_lon + o))
    return first, second


def lon_swaps(n_lat, n_lon):
    first = [(l * n_lon + o, l * n_lon + (o ^ 1)) for l in range(n_lat) for o in range(n_lon)]
    second = []
    for l in range(n_lat):
        for o in range(n_lon):
            other = (o + 1) % n_lon if o % 2 else (o - 1) % n_lon
            second.append((l * n_lon + o, l * n_lon + other))
    return first, second


def fold_gather(mine, other, n_lat, n_lon):
    buf = jnp.stack([mine, other])
    bit = 2
    top = n_lat - 1
    while bit < n_lon:
        pairs = [(top * n_lon + o, top * n_lon + (o ^ bit)) for o in range(n_lon)]
        buf = jnp.concatenate([buf, lax.ppermute(buf, AXES, pairs)])
        bit *= 2
    return buf


def stages(n_lat, n_lon):
    out = [[(1, 0)]]
    rest = [(1 << b, 0) for b in range(1, n_lat.bit_length() - 1)] + [(0, 1 << b) for b in range(n_lon.bit_length() - 1)]
    while rest:
        out.append(rest[:2])
        rest = rest[2:]
    return out


def group_index(group, lat, lon):
    value = jnp.int32(0)
    for ml, mo in group:
        bit = (lat & ml) != 0 if ml else (lon & mo) != 0
        value = 2 * value + bit.astype(jnp.int32)
    return value


def group_masks(group):
    masks = []
    for d in range(1 << len(group)):
        ml = mo = 0
        for k, (gl, go) in enumerate(group):
            if d >> (len(group) - 1 - k) & 1:
                ml, mo = ml | gl, mo | go
        masks.append((ml, mo))
    return masks


def all_sum(x, lat, lon, n_lat, n_lon):
    groups = stages(n_lat, n_lon)
    for group in groups:
        n = 1 << len(group)
        x = x.reshape((n, x.shape[0] // n) + x.shape[1:])
        idx = group_index(group, lat, lon)
        masks = group_masks(group)
        got = []
        for d in range(1, n):
            piece = lax.dynamic_index_in_dim(x, idx ^ d, 0, False)
            got.append(lax.ppermute(piece, AXES, swaps(n_lat, n_lon, masks[d])))
        total = lax.dynamic_index_in_dim(x, idx, 0, False).astype(F32)
        for g in got:
            total = total + g.astype(F32)
        x = total.astype(BF16)
    for group in reversed(groups):
        masks = group_masks(group)
        x = jnp.concatenate(
            [x] + [lax.ppermute(x, AXES, swaps(n_lat, n_lon, masks[d])) for d in range(1, len(masks))], axis=0
        )
    return x


def body(field_in, sea_mask, mirror, kernel, norm_gain, proj_in, proj_out, cotangent):
    nrows, ncols, width = field_in.shape
    hidden = proj_in.shape[1]
    n_lat, n_lon = lax.axis_size("lat"), lax.axis_size("lon")
    assert ncols == COLS and nrows % 16 == 0 and n_lat % 2 == 0 and n_lon % 2 == 0
    lat, lon = lax.axis_index("lat"), lax.axis_index("lon")
    cells = nrows * ncols
    tt = nrows // SUB
    groups = stages(n_lat, n_lon)
    me = jnp.int32(0)
    for group in groups:
        me = (me << len(group)) + group_index(group, lat, lon)
    sc = jnp.stack(
        [1 - lon % 2, 1 - lat % 2, (lat == n_lat - 1).astype(jnp.int32), lon, lon * ncols, me, jnp.int32(0), jnp.int32(0)]
    ).astype(jnp.int32)
    hp = -(-hidden // HB) * HB
    win = jnp.pad(proj_in, ((0, CP - width), (0, hp - hidden)))
    wout = jnp.pad(proj_out, ((0, hp - hidden), (0, CP - width)))
    gain = jnp.pad(norm_gain, (0, CP - width)).reshape(1, CP)

    s = jax.ShapeDtypeStruct
    row_msg = s((3, COLS, CP), BF16)
    strip_msg = s((LT, 3 * tt * 8 + 32, 128), BF16)
    mf, bk, mk, p1, p2 = pl.pallas_call(
        prepare_kernel,
        out_shape=(s((LT, cells, 128), F32), s((cells, CP), BF16), s((cells, 128), F32), row_msg, row_msg),
        in_specs=[SM, VM, VM, VM],
        out_specs=(VM,) * 5,
        scratch_shapes=[
            pltpu.VMEM((nrows, COLS, CP), BF16),
            pltpu.VMEM((6, COLS, CP), F32),
            pltpu.VMEM((LT, cells, 128), F32),
        ],
        compiler_params=params(),
        name="prepare",
    )(sc, sea_mask, field_in, cotangent)

    lat1, lat2 = lat_swaps(n_lat, n_lon)
    lon1, lon2 = lon_swaps(n_lat, n_lon)

    def halo(x, own1, own2):
        r1 = lax.ppermute(own1, AXES, lat1)
        r2 = lax.ppermute(own2, AXES, lat2)
        q1, q2 = pl.pallas_call(
            strips_kernel,
            out_shape=(strip_msg, strip_msg),
            in_specs=[SM, VM, VM, VM],
            out_specs=(VM, VM),
            scratch_shapes=[pltpu.VMEM((LT, 64, 128), F32)],
            compiler_params=params(),
            name="strips",
        )(sc, x, r1, r2)
        c1 = lax.ppermute(q1, AXES, lon1)
        c2 = lax.ppermute(q2, AXES, lon2)
        return c1, c2, r1, r2, fold_gather(own2, r2, n_lat, n_lon)

    halos = halo(mf, p1, p2)
    blocks = hp // 128
    count = 2 * blocks * (DWR // 16)
    out, ext, gc, g1, g2, dw, dgain = pl.pallas_call(
        lambda *refs: block_kernel(width, *refs),
        out_shape=(
            s((nrows, COLS, width), BF16),
            s((LT, (tt + 6) * QC * 8, 128), F32),
            s((LT, cells, 128), F32),
            row_msg,
            row_msg,
            s((count, 16, 128), BF16),
            s((8, CP), F32),
        ),
        in_specs=[SM, SM] + [VM] * 12,
        out_specs=(VM,) * 7,
        scratch_shapes=[
            pltpu.VMEM((LT, 56, 128), F32),
            pltpu.VMEM((LT, n_lon * 24, 128), F32),
            pltpu.VMEM((cells, CP), F32),
            pltpu.VMEM((cells, CP), BF16),
            pltpu.VMEM((cells, hp), BF16),
            pltpu.VMEM((cells, hp), BF16),
            pltpu.VMEM((LT, cells, 128), F32),
            pltpu.VMEM((6, COLS, CP), F32),
        ],
        compiler_params=params(),
        name="block",
    )(sc, mirror, kernel, gain, win, wout, mf, bk, mk, *halos)

    ghalos = halo(gc, g1, g2)
    dk = pl.pallas_call(
        taps_kernel,
        out_shape=s((LT * DKR // 16, 16, 128), BF16),
        in_specs=[VM] * 3,
        out_specs=VM,
        scratch_shapes=[pltpu.VMEM((LT, 49 * 8, 128), F32), pltpu.VMEM((LT, DKR, 128), F32)],
        compiler_params=params(),
        name="taps",
    )(ext, gc, dgain)
    grad_field = pl.pallas_call(
        lambda *refs: field_kernel(width, *refs),
        out_shape=s((nrows, COLS, width), BF16),
        in_specs=[SM, SM] + [VM] * 9,
        out_specs=VM,
        scratch_shapes=[
            pltpu.VMEM((LT, 56, 128), F32),
            pltpu.VMEM((LT, n_lon * 24, 128), F32),
            pltpu.VMEM((LT, (tt + 6) * QC * 8, 128), F32),
            pltpu.VMEM((LT, 3 * QC * 8, 128), F32),
            pltpu.VMEM((LT, cells, 128), F32),
        ],
        compiler_params=params(),
        name="field",
    )(sc, mirror, kernel, gc, bk, mk, *ghalos)

    devices = n_lat * n_lon
    used = count + LT * DKR // 16
    per = -(-used // devices)
    packed = jnp.concatenate([dw, dk, jnp.zeros((per * devices - used, 16, 128), BF16)], axis=0)
    summed = all_sum(packed, lat, lon, n_lat, n_lon)
    factor = float(1.0 / np.sqrt(np.float32(nrows * n_lat * ncols * n_lon)))
    gin, gout, gk, gg = pl.pallas_call(
        lambda *refs: unpack_kernel(width, hidden, factor, per, *refs),
        out_shape=(s((width, hidden), F32), s((hidden, width), F32), s((49, width), F32), s((1, width), F32)),
        in_specs=[SM, VM],
        out_specs=(VM,) * 4,
        compiler_params=params(),
        name="unpack",
    )(sc, summed)
    return out, grad_field, gin, gout, gk, gg.reshape(width)


def solution(mesh):
    in_specs = (
        P("lat", "lon", None),
        P("lat", "lon"),
        P(),
        P(),
        P(),
        P(),
        P(),
        P("lat", "lon", None),
    )
    out_specs = (P("lat", "lon", None), P("lat", "lon", None), P(), P(), P(), P())
    return jax.shard_map(body, mesh=mesh, in_specs=in_specs, out_specs=out_specs, check_vma=False)
```

```python
import jax
import jax.numpy as jnp
import numpy as np
from jax import lax
from jax.experimental import pallas as pl
from jax.experimental.pallas import tpu as pltpu
from jax.sharding import PartitionSpec as P

F32 = jnp.float32
BF16 = jnp.bfloat16
AXES = ("lat", "lon")
SUB = 8
COLS = 8
QC = COLS + 6
LT = 3
CP = LT * 128
HB = 256
VM = pl.BlockSpec(memory_space=pltpu.VMEM)
SM = pl.BlockSpec(memory_space=pltpu.SMEM)

EVEN_LON, EVEN_LAT, IS_TOP, LON, START, ME = range(6)


def cost(us):
    return pl.CostEstimate(flops=int(us * 1e6), bytes_accessed=int(us * 2e6), transcendentals=0)


def params(mib=60):
    return pltpu.CompilerParams(vmem_limit_bytes=mib * 1024 * 1024)


def lanes(l, width):
    return min(128, width - 128 * l)


def tap_rows(k_ref, ks, width):
    ks[...] = jnp.zeros_like(ks)
    for l in range(LT):
        w = lanes(l, width)
        ks[l, : k_ref.shape[0], :w] = k_ref[:, 128 * l : 128 * l + w]


def to_cells(src, l, i, put):
    x = src[pl.ds(l * 1024 + i, 128, stride=8), :].T
    for s in range(SUB):
        for t in (0, 8):
            put(pl.ds(t * 64 + i * 8 + s, 8, stride=64), x[16 * s + t : 16 * s + t + 8])


def to_channels(src, dst):
    for l in range(LT):
        for i in range(COLS):
            parts = [src[l, pl.ds(t * 64 + i * 8 + s, 8, stride=64), :] for s in range(SUB) for t in (0, 8)]
            dst[pl.ds(l * 1024 + i, 128, stride=8), :] = jnp.concatenate(parts, axis=0).T


def row_messages(sc, x_ref, rows, p1_ref, p2_ref):
    tt = x_ref.shape[1] // 64
    for l in range(LT):
        for r in range(3):
            rows[r, :, 128 * l : 128 * (l + 1)] = x_ref[l, pl.ds(r * 64, 8, stride=8), :]
            rows[3 + r, :, 128 * l : 128 * (l + 1)] = x_ref[l, pl.ds((tt - 3 + r) * 64 + 7, 8, stride=8), :]
    even = sc[EVEN_LAT]
    p1_ref[...] = rows[pl.ds(3 * even, 3)].astype(BF16)
    p2_ref[...] = rows[pl.ds(3 - 3 * even, 3)].astype(BF16)


def strip_messages(sc, x_ref, q1_ref, q2_ref):
    tt = x_ref.shape[1] // 64
    even = sc[EVEN_LON]
    for q_ref, first in ((q1_ref, 5 * even), (q2_ref, 5 - 5 * even)):
        for l in range(LT):
            for c in range(3):
                for t in range(0, tt, 2):
                    a = x_ref[l, pl.ds(pl.multiple_of(t * 64 + (first + c) * 8, 8), 8), :]
                    b = x_ref[l, pl.ds(pl.multiple_of(t * 64 + 64 + (first + c) * 8, 8), 8), :]
                    q_ref[l, (c * tt + t) * 8 : (c * tt + t) * 8 + 16, :] = jnp.concatenate([a, b], 0).astype(BF16)


def prepare_kernel(sc, mask_ref, f_ref, c_ref, mf_ref, bk_ref, q1_ref, q2_ref, p1_ref, p2_ref, cm, rows, ct):
    width = f_ref.shape[0]
    m = mask_ref[...].astype(F32)[None]
    cm[width * 8 :, :] = jnp.zeros((cm.shape[0] - width * 8, 128), F32)
    for src, dst in ((f_ref, mf_ref), (c_ref, ct)):
        cm[: width * 8, :] = (src[...].astype(F32) * m).reshape(width * 8, 128)
        for l in range(LT):
            for i in range(COLS):

                def put(at, v, l=l, dst=dst):
                    dst[l, at, :] = v

                to_cells(cm, l, i, put)
    strip_messages(sc, mf_ref, q1_ref, q2_ref)
    row_messages(sc, mf_ref, rows, p1_ref, p2_ref)
    for l in range(LT):
        bk_ref[:, 128 * l : 128 * (l + 1)] = ct[l].astype(BF16)


def extend(sc, ext, x_ref, q1_ref, q2_ref, p1_ref, p2_ref, c1_ref, c2_ref):
    tt = x_ref.shape[1] // 64
    even_lat, even_lon, top = sc[EVEN_LAT], sc[EVEN_LON], sc[IS_TOP]
    for l in range(LT):
        for t in range(tt):
            ext[l, ((t + 3) * QC + 3) * 8 : ((t + 3) * QC + 3) * 8 + 64, :] = x_ref[l, t * 64 : t * 64 + 64, :]
    sides = ((q1_ref, c1_ref, even_lon), (q2_ref, c2_ref, 1 - even_lon))
    for q_ref, _, right in sides:
        for l in range(LT):
            for c in range(3):
                for t in range(0, tt, 2):
                    v = q_ref[l, (c * tt + t) * 8 : (c * tt + t) * 8 + 16, :].astype(F32)
                    for u in range(2):
                        at = ((t + u + 3) * QC + 11 * right + c) * 8
                        ext[l, pl.ds(pl.multiple_of(at, 8), 8), :] = v[8 * u : 8 * u + 8]
    for l in range(LT):
        for r in range(3):
            for q in range(QC):
                lo = ext[l, ((tt + r) * QC + q) * 8 : ((tt + r) * QC + q) * 8 + 8, :]
                ext[l, (r * QC + q) * 8 : (r * QC + q) * 8 + 8, :] = pltpu.roll(lo, 1, 0)
                hi = ext[l, ((3 + r) * QC + q) * 8 : ((3 + r) * QC + q) * 8 + 8, :]
                at = ((tt + 3 + r) * QC + q) * 8
                ext[l, at : at + 8, :] = pltpu.roll(hi, 7, 0)
    keep = (1 - top).astype(F32)
    p1, p2 = p1_ref[...].astype(F32), p2_ref[...].astype(F32)
    lower = jnp.where(even_lat == 1, p2, p1)
    upper = jnp.where(even_lat == 1, p1, p2) * keep
    for l in range(LT):
        for r in range(3):
            ext[l, pl.ds((r * QC + 3) * 8, 8, stride=8), :] = lower[r, :, 128 * l : 128 * (l + 1)]
            ext[l, pl.ds(((tt + 3 + r) * QC + 3) * 8 + 7, 8, stride=8), :] = upper[r, :, 128 * l : 128 * (l + 1)]
    for _, c_ref, right in sides:
        first = 11 * right
        for r in range(3):
            lo = c_ref[even_lat, r].astype(F32)
            up = c_ref[1 - even_lat, r].astype(F32) * keep
            for c in range(3):
                lo_row = jnp.where(right == 1, lo[c : c + 1], lo[5 + c : 6 + c])
                up_row = jnp.where(right == 1, up[c : c + 1], up[5 + c : 6 + c])
                for l in range(LT):
                    ext[l, pl.ds((r * QC + first + c) * 8, 1), :] = lo_row[:, 128 * l : 128 * (l + 1)]
                    at = ((tt + 3 + r) * QC + first + c) * 8 + 7
                    ext[l, pl.ds(at, 1), :] = up_row[:, 128 * l : 128 * (l + 1)]


def fold_rows(sc, mir, fold_refs, buf, dst, base):
    first = 0
    for ref in fold_refs:
        for u in range(ref.shape[0]):
            for r in range(3):
                at = ((first + u) * 3 + r) * 8
                v = ref[u, r].astype(F32)
                for l in range(LT):
                    buf[l, at : at + 8, :] = v[:, 128 * l : 128 * (l + 1)]
        first += ref.shape[0]
    total = mir.shape[0]
    for q in range(QC):
        col = sc[START] - 3 + q
        col = jnp.where(col < 0, col + total, col)
        col = jnp.where(col >= total, col - total, col)
        m = mir[col]
        unit = lax.shift_right_logical(m, 3) - sc[LON] + 1 + sc[EVEN_LON]
        unit = jnp.where(unit < 0, unit + first, unit)
        unit = jnp.where(unit >= first, unit - first, unit)
        at = unit * 24 + lax.bitwise_and(m, 7)
        for k in range(3):
            for l in range(LT):
                dst[l, pl.ds(base + (k * QC + q) * 8 + 7, 1), :] = buf[l, pl.ds(at + (2 - k) * 8, 1), :]


def correlate(ext, ks, tt, flip, store):
    for l in range(LT):

        def column(i, carry, l=l):
            acc = [None] * tt
            for b in range(7):
                k = []
                for a in range(7):
                    tap = 7 * a + b
                    tap = 48 - tap if flip else tap
                    k.append(jnp.broadcast_to(ks[l, tap : tap + 1, :], (8, 128)))
                for u in range(tt + 6):
                    e = ext[l, pl.ds(pl.multiple_of((u * QC + i + b) * 8, 8), 8), :]
                    for a in range(7):
                        t = u - a
                        if 0 <= t < tt:
                            v = k[a] * e
                            acc[t] = v if acc[t] is None else acc[t] + v
            for t in range(tt):
                store(l, t, i, acc[t])
            return carry

        lax.fori_loop(0, COLS, column, 0)


DWR = 304
DKR = 64


def block_kernel(width, nf, sc, mir, k_ref, gain_ref, win_ref, wout_ref, mask_ref, f_ref, mf_ref, bk_ref, *refs):
    halos, folds = refs[:6], refs[6 : 6 + nf]
    out_ref, ext, gc_ref, q1_ref, q2_ref, g1_ref, g2_ref, dw_ref, dgain_ref = refs[6 + nf : 15 + nf]
    ks, buf, conv, normed, act, gp, res, rows, cm = refs[15 + nf :]
    cells = mf_ref.shape[1]
    tt = cells // 64
    hidden = win_ref.shape[1]
    extend(sc, ext, mf_ref, *halos)

    @pl.when(sc[IS_TOP] == 1)
    def _():
        fold_rows(sc, mir, folds, buf, ext, (tt + 3) * QC * 8)

    tap_rows(k_ref, ks, width)

    def put(l, t, i, v):
        conv[pl.ds(pl.multiple_of(t * 64 + i * 8, 8), 8), 128 * l : 128 * (l + 1)] = v

    correlate(ext, ks, tt, False, put)
    size = 256
    gain = gain_ref[...]
    valid = (lax.broadcasted_iota(jnp.int32, (1, CP), 1) < width).astype(F32)
    dgain_ref[...] = jnp.zeros_like(dgain_ref)
    inv = 1.0 / width
    coeff = 0.7978845608028654
    nt = (((1,), (1,)), ((), ()))

    def chunk(n, carry):
        at = pl.ds(pl.multiple_of(n * size, size), size)
        x = conv[at, :]
        mean = jnp.sum(x, axis=-1, keepdims=True) * inv
        cen = (x - mean) * valid
        var = jnp.sum(cen * cen, axis=-1, keepdims=True) * inv
        rstd = lax.rsqrt(var + 1e-06)
        nhat = cen * rstd
        nb = (nhat * gain).astype(BF16)
        normed[at, :] = nb
        back = bk_ref[at, :]
        for h in range(0, hidden, HB):
            v = jnp.dot(nb, win_ref[:, h : h + HB], preferred_element_type=F32)
            g = jnp.dot(back, wout_ref[:, h : h + HB], preferred_element_type=F32)
            v2 = v * v
            half = 0.5 + 0.5 * jnp.tanh(v * (coeff + (coeff * 0.044715) * v2))
            a = v * half
            slope = half + a * (1.0 - half) * (2.0 * coeff + (2.0 * coeff * 0.134145) * v2)
            act[at, h : h + HB] = a.astype(BF16)
            gp[at, h : h + HB] = (g * slope).astype(BF16)
        mixed = lax.dot_general(act[at, :], wout_ref[...], nt, preferred_element_type=F32)
        gn = lax.dot_general(gp[at, :], win_ref[...], nt, preferred_element_type=F32)
        for l in range(LT):
            res[l, at, :] = mixed[:, 128 * l : 128 * (l + 1)]
        dgain_ref[...] += jnp.broadcast_to(jnp.sum(gn * nhat, axis=0, keepdims=True), dgain_ref.shape)
        s = gn * gain
        m1 = jnp.sum(s, axis=-1, keepdims=True) * inv
        m2 = jnp.sum(s * nhat, axis=-1, keepdims=True) * inv
        gc = (rstd * (s - m1 - nhat * m2) * valid).astype(BF16).astype(F32)
        for l in range(LT):
            gc_ref[l, at, :] = gc[:, 128 * l : 128 * (l + 1)]
        return carry

    lax.fori_loop(0, cells // size, chunk, 0)
    strip_messages(sc, gc_ref, q1_ref, q2_ref)
    row_messages(sc, gc_ref, rows, g1_ref, g2_ref)
    tiles = (hidden // 128) * (DWR // 16)
    for m, (left, right) in enumerate(((normed, gp), (bk_ref, act))):
        for h in range(0, hidden, HB):
            d = lax.dot_general(
                left[...], right[:, h : h + HB], (((0,), (0,)), ((), ())), preferred_element_type=F32
            ).astype(BF16)
            for u in range(HB // 128):
                first = m * tiles + (h // 128 + u) * (DWR // 16)
                for r in range(DWR // 16):
                    dw_ref[first + r] = d[16 * r : 16 * r + 16, 128 * u : 128 * u + 128]
    dw_ref[2 * tiles :] = jnp.zeros((dw_ref.shape[0] - 2 * tiles, 16, 128), BF16)
    to_channels(res, cm)
    mixed = cm[: width * 8, :].reshape(width, 8, 128)
    out_ref[...] = (mask_ref[...].astype(F32)[None] * (f_ref[...].astype(F32) + mixed)).astype(BF16)


def taps_kernel(count, ext, gc_ref, dgain_ref, dw_ref, dk_ref, part, rows, tiles, sem):
    tt = gc_ref.shape[1] // 64
    for l in range(LT):

        def tap_column(b, carry, l=l):
            acc = [[None, None] for _ in range(7)]
            for i in range(COLS):
                g = [gc_ref[l, t * 64 + i * 8 : t * 64 + i * 8 + 8, :] for t in range(tt)]
                for u in range(tt + 6):
                    e = ext[l, pl.ds(pl.multiple_of((u * QC + i + b) * 8, 8), 8), :]
                    for a in range(7):
                        t = u - a
                        if 0 <= t < tt:
                            v = g[t] * e
                            acc[a][u % 2] = v if acc[a][u % 2] is None else acc[a][u % 2] + v
            for a in range(7):
                part[l, pl.ds(pl.multiple_of((7 * a + b) * 8, 8), 8), :] = acc[a][0] + acc[a][1]
            return carry

        lax.fori_loop(0, 7, tap_column, 0)
    rows[...] = jnp.zeros_like(rows)
    for l in range(LT):
        for k in range(49):
            rows[l, k : k + 1, :] = jnp.sum(part[l, 8 * k : 8 * k + 8, :], axis=0, keepdims=True)
        rows[l, 49:50, :] = dgain_ref[0:1, 128 * l : 128 * (l + 1)]
        for r in range(DKR // 16):
            tiles[l * (DKR // 16) + r] = rows[l, 16 * r : 16 * r + 16, :].astype(BF16)
    copy = pltpu.make_async_copy(tiles, dk_ref.at[pl.ds(count, LT * (DKR // 16))], sem)
    copy.start()
    copy.wait()


def field_kernel(width, nf, sc, mir, k_ref, mask_ref, c_ref, gc_ref, *refs):
    halos, folds = refs[:6], refs[6 : 6 + nf]
    out_ref, ks, buf, ext, ghost, dm, cm = refs[6 + nf :]
    cells = gc_ref.shape[1]
    tt = cells // 64
    extend(sc, ext, gc_ref, *halos)
    tap_rows(k_ref, ks, width)

    def put(l, t, i, v):
        dm[l, pl.ds(pl.multiple_of(t * 64 + i * 8, 8), 8), :] = v

    correlate(ext, ks, tt, True, put)

    @pl.when(sc[IS_TOP] == 1)
    def _():
        ghost[...] = jnp.zeros_like(ghost)
        fold_rows(sc, mir, folds, buf, ghost, 0)
        for l in range(LT):

            def column(i, carry, l=l):
                for k in range(3):
                    at = pl.ds(pl.multiple_of((tt - 1 - k) * 64 + i * 8, 8), 8)
                    acc = dm[l, at, :]
                    for r in range(3 - k):
                        for b in range(7):
                            tap = 7 * (4 + k + r) + b
                            e = ghost[l, pl.ds(pl.multiple_of((r * QC + i + b) * 8, 8), 8), :]
                            acc = acc + jnp.broadcast_to(ks[l, tap : tap + 1, :], (8, 128)) * e
                    dm[l, at, :] = acc
                return carry

            lax.fori_loop(0, COLS, column, 0)

    to_channels(dm, cm)
    total = cm[: width * 8, :].reshape(width, 8, 128)
    out_ref[...] = (mask_ref[...].astype(F32)[None] * (c_ref[...].astype(F32) + total)).astype(BF16)


def unpack_kernel(width, hidden, factor, per, sc, x_ref, gin_ref, gout_ref, gk_ref, gg_ref):
    blocks = (hidden + 127) // 128
    blocks += blocks % 2
    tr = DWR // 16

    def tile(n):
        chunk = lax.bitwise_xor(jnp.int32(n // per), sc[ME])
        return x_ref[chunk * per + n % per].astype(F32) * factor

    for cb in range(blocks):
        w = min(128, hidden - 128 * cb)
        if w <= 0:
            continue
        for r in range(tr):
            rows = min(16, width - 16 * r)
            gin_ref[16 * r : 16 * r + rows, 128 * cb : 128 * cb + w] = tile(cb * tr + r)[:rows, :w]
            gout_ref[16 * r : 16 * r + rows, 128 * cb : 128 * cb + w] = tile((blocks + cb) * tr + r)[:rows, :w]
    for l in range(LT):
        w = lanes(l, width)
        base = 2 * blocks * tr + l * (DKR // 16)
        taps = jnp.concatenate([tile(base + r) for r in range(DKR // 16)], axis=0)
        gk_ref[:, 128 * l : 128 * l + w] = taps[:49, :w]
        gg_ref[:, 128 * l : 128 * l + w] = taps[49:50, :w]


def swaps(n_lat, n_lon, bits):
    ml, mo = bits
    return [(l * n_lon + o, (l ^ ml) * n_lon + (o ^ mo)) for l in range(n_lat) for o in range(n_lon)]


def lat_swaps(n_lat, n_lon):
    first = [(l * n_lon + o, (l ^ 1) * n_lon + o) for l in range(n_lat) for o in range(n_lon)]
    second = []
    for l in range(n_lat):
        for o in range(n_lon):
            if l == n_lat - 1:
                second.append((l * n_lon + o, l * n_lon + (o ^ 1)))
            elif l > 0:
                other = l + 1 if l % 2 else l - 1
                second.append((l * n_lon + o, other * n_lon + o))
    return first, second


def lon_swaps(n_lat, n_lon):
    first = [(l * n_lon + o, l * n_lon + (o ^ 1)) for l in range(n_lat) for o in range(n_lon)]
    second = []
    for l in range(n_lat):
        for o in range(n_lon):
            other = (o + 1) % n_lon if o % 2 else (o - 1) % n_lon
            second.append((l * n_lon + o, l * n_lon + other))
    return first, second


def fold_gather(own, pair, c2, even_lon, n_lat, n_lon):
    up = jnp.stack([c2[1], c2[2], own, pair])
    down = jnp.stack([pair, own, c2[2], c2[1]])
    units = [jnp.where(even_lon, up, down)]
    top = n_lat - 1
    step = 4
    while step < n_lon:
        have = jnp.concatenate(units) if len(units) > 1 else units[0]
        pairs = [(top * n_lon + (o + step) % n_lon, top * n_lon + o) for o in range(n_lon)]
        units.append(lax.ppermute(have, AXES, pairs))
        step *= 2
    return units


def stages(n_lat, n_lon):
    out = [[(1, 0)]]
    rest = [(1 << b, 0) for b in range(1, n_lat.bit_length() - 1)] + [(0, 1 << b) for b in range(n_lon.bit_length() - 1)]
    while rest:
        out.append(rest[:2])
        rest = rest[2:]
    return out


def group_index(group, lat, lon):
    value = jnp.int32(0)
    for ml, mo in group:
        bit = (lat & ml) != 0 if ml else (lon & mo) != 0
        value = 2 * value + bit.astype(jnp.int32)
    return value


def group_masks(group):
    masks = []
    for d in range(1 << len(group)):
        ml = mo = 0
        for k, (gl, go) in enumerate(group):
            if d >> (len(group) - 1 - k) & 1:
                ml, mo = ml | gl, mo | go
        masks.append((ml, mo))
    return masks


def all_sum(x, beside, lat, lon, n_lat, n_lon):
    groups = stages(n_lat, n_lon)
    for k, group in enumerate(groups):
        n = 1 << len(group)
        x = x.reshape((n, x.shape[0] // n) + x.shape[1:])
        idx = group_index(group, lat, lon)
        masks = group_masks(group)
        got = []
        for d in range(1, n):
            piece = lax.dynamic_index_in_dim(x, idx ^ d, 0, False)
            got.append(lax.ppermute(piece, AXES, swaps(n_lat, n_lon, masks[d])))
        if k == 1:
            got, beside = lax.optimization_barrier((got, beside))
        total = lax.dynamic_index_in_dim(x, idx, 0, False).astype(F32)
        for g in got:
            total = total + g.astype(F32)
        x = total.astype(BF16)
    for group in reversed(groups):
        masks = group_masks(group)
        x = jnp.concatenate(
            [x] + [lax.ppermute(x, AXES, swaps(n_lat, n_lon, masks[d])) for d in range(1, len(masks))], axis=0
        )
    return x, beside


def body(field_in, sea_mask, mirror, kernel, norm_gain, proj_in, proj_out, cotangent):
    nrows, ncols, width = field_in.shape
    hidden = proj_in.shape[1]
    n_lat, n_lon = lax.axis_size("lat"), lax.axis_size("lon")
    assert ncols == COLS and nrows % 16 == 0 and n_lat % 2 == 0 and n_lon % 2 == 0
    lat, lon = lax.axis_index("lat"), lax.axis_index("lon")
    cells = nrows * ncols
    tt = nrows // SUB
    groups = stages(n_lat, n_lon)
    me = jnp.int32(0)
    for group in groups:
        me = (me << len(group)) + group_index(group, lat, lon)
    sc = jnp.stack(
        [1 - lon % 2, 1 - lat % 2, (lat == n_lat - 1).astype(jnp.int32), lon, lon * ncols, me, jnp.int32(0), jnp.int32(0)]
    ).astype(jnp.int32)
    assert nrows == 128 and n_lon % 4 == 0
    hp = -(-hidden // HB) * HB
    win = jnp.pad(proj_in, ((0, CP - width), (0, hp - hidden)))
    wout = jnp.pad(proj_out.T, ((0, CP - width), (0, hp - hidden)))
    gain = jnp.pad(norm_gain, (0, CP - width)).reshape(1, CP)
    field_c = field_in.transpose(2, 1, 0)
    cot_c = cotangent.transpose(2, 1, 0)
    mask_c = sea_mask.T

    s = jax.ShapeDtypeStruct
    row_msg = s((3, COLS, CP), BF16)
    strip_msg = s((LT, 3 * tt * 8, 128), BF16)
    channels = pltpu.VMEM((CP * 8, 128), F32)
    mf, bk, q1, q2, p1, p2 = pl.pallas_call(
        prepare_kernel,
        out_shape=(s((LT, cells, 128), F32), s((cells, CP), BF16), strip_msg, strip_msg, row_msg, row_msg),
        in_specs=[SM, VM, VM, VM],
        out_specs=(VM,) * 6,
        scratch_shapes=[channels, pltpu.VMEM((6, COLS, CP), F32), pltpu.VMEM((LT, cells, 128), F32)],
        compiler_params=params(9),
        name="prepare",
        cost_estimate=cost(5),
    )(sc, mask_c, field_c, cot_c)

    lat1, lat2 = lat_swaps(n_lat, n_lon)
    lon1, lon2 = lon_swaps(n_lat, n_lon)

    def halo(q1, q2, p1, p2):
        s1 = lax.ppermute(q1, AXES, lon1)
        s2 = lax.ppermute(q2, AXES, lon2)
        r1 = lax.ppermute(p1, AXES, lat1)
        r2 = lax.ppermute(p2, AXES, lat2)
        rows = jnp.stack([r1, r2, p2])
        c1 = lax.ppermute(rows, AXES, lon1)
        c2 = lax.ppermute(rows, AXES, lon2)
        folds = fold_gather(p2, r2, c2, lon % 2 == 0, n_lat, n_lon)
        return [s1, s2, r1, r2, c1, c2] + folds, rows

    halos, _ = halo(q1, q2, p1, p2)
    nf = len(halos) - 6
    count = 2 * (hp // 128) * (DWR // 16)
    devices = n_lat * n_lon
    per = -(-(count + LT * DKR // 16) // devices)
    out, ext, gc, q1, q2, g1, g2, dw, dgain = pl.pallas_call(
        lambda *refs: block_kernel(width, nf, *refs),
        out_shape=(
            s((width, COLS, nrows), BF16),
            s((LT, (tt + 6) * QC * 8, 128), F32),
            s((LT, cells, 128), F32),
            strip_msg,
            strip_msg,
            row_msg,
            row_msg,
            s((per * devices, 16, 128), BF16),
            s((8, CP), F32),
        ),
        in_specs=[SM, SM] + [VM] * (len(halos) + 8),
        out_specs=(VM,) * 9,
        scratch_shapes=[
            pltpu.VMEM((LT, 56, 128), F32),
            pltpu.VMEM((LT, n_lon * 24, 128), F32),
            pltpu.VMEM((cells, CP), F32),
            pltpu.VMEM((cells, CP), BF16),
            pltpu.VMEM((cells, hp), BF16),
            pltpu.VMEM((cells, hp), BF16),
            pltpu.VMEM((LT, cells, 128), F32),
            pltpu.VMEM((6, COLS, CP), F32),
            channels,
        ],
        compiler_params=params(20),
        name="block",
        cost_estimate=cost(20),
    )(sc, mirror, kernel, gain, win, wout, mask_c, field_c, mf, bk, *halos)

    ghalos, rows = halo(q1, q2, g1, g2)
    gc_late, _ = lax.optimization_barrier((gc, rows))
    packed = pl.pallas_call(
        lambda *refs: taps_kernel(count, *refs),
        out_shape=s((per * devices, 16, 128), BF16),
        in_specs=[VM] * 3 + [pl.BlockSpec(memory_space=pl.ANY)],
        out_specs=pl.BlockSpec(memory_space=pl.ANY),
        scratch_shapes=[
            pltpu.VMEM((LT, 49 * 8, 128), F32),
            pltpu.VMEM((LT, DKR, 128), F32),
            pltpu.VMEM((LT * DKR // 16, 16, 128), BF16),
            pltpu.SemaphoreType.DMA,
        ],
        input_output_aliases={3: 0},
        compiler_params=params(6),
        name="taps",
        cost_estimate=cost(9),
    )(ext, gc_late, dgain, dw)
    grad_field = pl.pallas_call(
        lambda *refs: field_kernel(width, nf, *refs),
        out_shape=s((width, COLS, nrows), BF16),
        in_specs=[SM, SM] + [VM] * (len(ghalos) + 4),
        out_specs=VM,
        scratch_shapes=[
            pltpu.VMEM((LT, 56, 128), F32),
            pltpu.VMEM((LT, n_lon * 24, 128), F32),
            pltpu.VMEM((LT, (tt + 6) * QC * 8, 128), F32),
            pltpu.VMEM((LT, 3 * QC * 8, 128), F32),
            pltpu.VMEM((LT, cells, 128), F32),
            channels,
        ],
        compiler_params=params(12),
        name="field",
        cost_estimate=cost(11),
    )(sc, mirror, kernel, mask_c, cot_c, gc, *ghalos)

    packed, _ = lax.optimization_barrier((packed, ghalos))
    summed, grad_field = all_sum(packed, grad_field, lat, lon, n_lat, n_lon)
    factor = float(1.0 / np.sqrt(np.float32(nrows * n_lat * ncols * n_lon)))
    gin, gout, gk, gg = pl.pallas_call(
        lambda *refs: unpack_kernel(width, hidden, factor, per, *refs),
        out_shape=(s((width, hidden), F32), s((width, hidden), F32), s((49, width), F32), s((1, width), F32)),
        in_specs=[SM, VM],
        out_specs=(VM,) * 4,
        compiler_params=params(8),
        name="unpack",
        cost_estimate=cost(4),
    )(sc, summed)
    return out.transpose(2, 1, 0), grad_field.transpose(2, 1, 0), gin, gout.T, gk, gg.reshape(width)


def solution(mesh):
    in_specs = (
        P("lat", "lon", None),
        P("lat", "lon"),
        P(),
        P(),
        P(),
        P(),
        P(),
        P("lat", "lon", None),
    )
    out_specs = (P("lat", "lon", None), P("lat", "lon", None), P(), P(), P(), P())
    return jax.shard_map(body, mesh=mesh, in_specs=in_specs, out_specs=out_specs, check_vma=False)
```

```python
import jax
import jax.numpy as jnp
import numpy as np
from jax import lax
from jax.experimental import pallas as pl
from jax.experimental.pallas import tpu as pltpu
from jax.sharding import PartitionSpec as P

F32 = jnp.float32
BF16 = jnp.bfloat16
AXES = ("lat", "lon")
SUB = 8
COLS = 8
QC = COLS + 6
LT = 3
CP = LT * 128
HB = 256
VM = pl.BlockSpec(memory_space=pltpu.VMEM)
SM = pl.BlockSpec(memory_space=pltpu.SMEM)
ANY = pl.BlockSpec(memory_space=pl.ANY)

EVEN_LON, EVEN_LAT, IS_TOP, LON, START, ME, CORE = range(7)


def cost(us):
    return pl.CostEstimate(flops=int(us * 1e6), bytes_accessed=int(us * 2e6), transcendentals=0)


def params(mib=60):
    return pltpu.CompilerParams(vmem_limit_bytes=mib * 1024 * 1024)


def lanes(l, width):
    return min(128, width - 128 * l)


def tap_rows(k_ref, ks, width):
    ks[...] = jnp.zeros_like(ks)
    for l in range(LT):
        w = lanes(l, width)
        ks[l, : k_ref.shape[0], :w] = k_ref[:, 128 * l : 128 * l + w]


def to_cells(src, l, i, put):
    x = src[pl.ds(l * 1024 + i, 128, stride=8), :].T
    for s in range(SUB):
        for t in (0, 8):
            put(pl.ds(t * 64 + i * 8 + s, 8, stride=64), x[16 * s + t : 16 * s + t + 8])


def to_channels(src, dst):
    for l in range(LT):
        for i in range(COLS):
            parts = [src[l, pl.ds(t * 64 + i * 8 + s, 8, stride=64), :] for s in range(SUB) for t in (0, 8)]
            dst[pl.ds(l * 1024 + i, 128, stride=8), :] = jnp.concatenate(parts, axis=0).T


def row_messages(sc, x_ref, rows, p1_ref, p2_ref):
    tt = x_ref.shape[1] // 64
    for l in range(LT):
        for r in range(3):
            rows[r, :, 128 * l : 128 * (l + 1)] = x_ref[l, pl.ds(r * 64, 8, stride=8), :]
            rows[3 + r, :, 128 * l : 128 * (l + 1)] = x_ref[l, pl.ds((tt - 3 + r) * 64 + 7, 8, stride=8), :]
    even = sc[EVEN_LAT]
    p1_ref[...] = rows[pl.ds(3 * even, 3)].astype(BF16)
    p2_ref[...] = rows[pl.ds(3 - 3 * even, 3)].astype(BF16)


def strip_messages(sc, x_ref, q1_ref, q2_ref):
    tt = x_ref.shape[1] // 64
    even = sc[EVEN_LON]
    for q_ref, first in ((q1_ref, 5 * even), (q2_ref, 5 - 5 * even)):
        for l in range(LT):
            for c in range(3):
                for t in range(0, tt, 2):
                    a = x_ref[l, pl.ds(pl.multiple_of(t * 64 + (first + c) * 8, 8), 8), :]
                    b = x_ref[l, pl.ds(pl.multiple_of(t * 64 + 64 + (first + c) * 8, 8), 8), :]
                    q_ref[l, (c * tt + t) * 8 : (c * tt + t) * 8 + 16, :] = jnp.concatenate([a, b], 0).astype(BF16)
            q_ref[l, 3 * tt * 8 :, :] = jnp.zeros((32, 128), BF16)


def corners_kernel(sc, p1_ref, p2_ref, _, __, q1_ref, q2_ref, lu, corner, sem):
    even_lat, even = sc[EVEN_LAT], sc[EVEN_LON]
    p1, p2 = p1_ref[...].astype(F32), p2_ref[...].astype(F32)
    lower = jnp.where(even_lat == 1, p2, p1)
    upper = jnp.where(even_lat == 1, p1, p2)
    for l in range(LT):
        for r in range(3):
            lu[l, 8 * r : 8 * r + 8, :] = lower[r, :, 128 * l : 128 * (l + 1)]
            lu[l, 24 + 8 * r : 32 + 8 * r, :] = upper[r, :, 128 * l : 128 * (l + 1)]
        lu[l, 48:, :] = jnp.zeros((16, 128), F32)
    copies = []
    for n, (q_ref, first) in enumerate(((q1_ref, 5 * even), (q2_ref, 5 - 5 * even))):
        for l in range(LT):
            k = [lu[l, pl.ds(first + c, 8, stride=8), :] for c in range(3)]
            k.append(jnp.zeros((8, 128), F32))
            corner[n, l] = jnp.concatenate(k, 0).astype(BF16)
        rows = q_ref.shape[1]
        copies.append(pltpu.make_async_copy(corner.at[n], q_ref.at[:, pl.ds(rows - 32, 32), :], sem.at[n]))
        copies[-1].start()
    for copy in copies:
        copy.wait()


def masked_cells(mask_ref, src, cm, dst):
    width = src.shape[0]
    m = mask_ref[...].astype(F32)[None]
    cm[width * 8 :, :] = jnp.zeros((cm.shape[0] - width * 8, 128), F32)
    cm[: width * 8, :] = (src[...].astype(F32) * m).reshape(width * 8, 128)
    for l in range(LT):
        for i in range(COLS):

            def put(at, v, l=l):
                dst[l, at, :] = v

            to_cells(cm, l, i, put)


def prepare_kernel(sc, mask_ref, f_ref, mf_ref, p1_ref, p2_ref, q1_ref, q2_ref, cm, rows):
    masked_cells(mask_ref, f_ref, cm, mf_ref)
    row_messages(sc, mf_ref, rows, p1_ref, p2_ref)
    strip_messages(sc, mf_ref, q1_ref, q2_ref)


def back_kernel(mask_ref, c_ref, bk_ref, cm, ct):
    masked_cells(mask_ref, c_ref, cm, ct)
    for l in range(LT):
        bk_ref[:, 128 * l : 128 * (l + 1)] = ct[l].astype(BF16)


def extend(sc, ext, x_ref, q1_ref, q2_ref, p1_ref, p2_ref):
    tt = x_ref.shape[1] // 64
    even_lat, even_lon, top = sc[EVEN_LAT], sc[EVEN_LON], sc[IS_TOP]
    for l in range(LT):
        for t in range(tt):
            ext[l, ((t + 3) * QC + 3) * 8 : ((t + 3) * QC + 3) * 8 + 64, :] = x_ref[l, t * 64 : t * 64 + 64, :]
    sides = ((q1_ref, even_lon), (q2_ref, 1 - even_lon))
    for q_ref, right in sides:
        for l in range(LT):
            for c in range(3):
                for t in range(0, tt, 2):
                    v = q_ref[l, (c * tt + t) * 8 : (c * tt + t) * 8 + 16, :].astype(F32)
                    for u in range(2):
                        at = ((t + u + 3) * QC + 11 * right + c) * 8
                        ext[l, pl.ds(pl.multiple_of(at, 8), 8), :] = v[8 * u : 8 * u + 8]
    for l in range(LT):
        for r in range(3):
            for q in range(QC):
                lo = ext[l, ((tt + r) * QC + q) * 8 : ((tt + r) * QC + q) * 8 + 8, :]
                ext[l, (r * QC + q) * 8 : (r * QC + q) * 8 + 8, :] = pltpu.roll(lo, 1, 0)
                hi = ext[l, ((3 + r) * QC + q) * 8 : ((3 + r) * QC + q) * 8 + 8, :]
                at = ((tt + 3 + r) * QC + q) * 8
                ext[l, at : at + 8, :] = pltpu.roll(hi, 7, 0)
    keep = (1 - top).astype(F32)
    p1, p2 = p1_ref[...].astype(F32), p2_ref[...].astype(F32)
    lower = jnp.where(even_lat == 1, p2, p1)
    upper = jnp.where(even_lat == 1, p1, p2) * keep
    for l in range(LT):
        for r in range(3):
            ext[l, pl.ds((r * QC + 3) * 8, 8, stride=8), :] = lower[r, :, 128 * l : 128 * (l + 1)]
            ext[l, pl.ds(((tt + 3 + r) * QC + 3) * 8 + 7, 8, stride=8), :] = upper[r, :, 128 * l : 128 * (l + 1)]
    for q_ref, right in sides:
        first = 11 * right
        for l in range(LT):
            corner = q_ref[l, 3 * tt * 8 : 3 * tt * 8 + 32, :].astype(F32)
            for c in range(3):
                for r in range(3):
                    ext[l, pl.ds((r * QC + first + c) * 8, 1), :] = corner[8 * c + r : 8 * c + r + 1]
                    at = ((tt + 3 + r) * QC + first + c) * 8 + 7
                    ext[l, pl.ds(at, 1), :] = corner[8 * c + 3 + r : 8 * c + 4 + r] * keep


def fold_rows(sc, mir, fold_refs, buf, dst, base):
    first = 0
    for ref in fold_refs:
        for u in range(ref.shape[0]):
            for r in range(3):
                at = ((first + u) * 3 + r) * 8
                v = ref[u, r].astype(F32)
                for l in range(LT):
                    buf[l, at : at + 8, :] = v[:, 128 * l : 128 * (l + 1)]
        first += ref.shape[0]
    total = mir.shape[0]
    for q in range(QC):
        col = sc[START] - 3 + q
        col = jnp.where(col < 0, col + total, col)
        col = jnp.where(col >= total, col - total, col)
        m = mir[col]
        unit = lax.bitwise_xor(lax.shift_right_logical(m, 3), sc[LON])
        at = unit * 24 + lax.bitwise_and(m, 7)
        for k in range(3):
            for l in range(LT):
                dst[l, pl.ds(base + (k * QC + q) * 8 + 7, 1), :] = buf[l, pl.ds(at + (2 - k) * 8, 1), :]


def extend_all(sc, mir, ext, buf, x_ref, halos, folds):
    extend(sc, ext, x_ref, *halos)

    @pl.when(sc[IS_TOP] == 1)
    def _():
        fold_rows(sc, mir, folds, buf, ext, (x_ref.shape[1] // 64 + 3) * QC * 8)


def correlate(ext, ks, tt, flip, store):
    for l in range(LT):

        def column(i, carry, l=l):
            acc = [None] * tt
            for b in range(7):
                k = []
                for a in range(7):
                    tap = 7 * a + b
                    tap = 48 - tap if flip else tap
                    k.append(jnp.broadcast_to(ks[l, tap : tap + 1, :], (8, 128)))
                for u in range(tt + 6):
                    e = ext[l, pl.ds(pl.multiple_of((u * QC + i + b) * 8, 8), 8), :]
                    for a in range(7):
                        t = u - a
                        if 0 <= t < tt:
                            v = k[a] * e
                            acc[t] = v if acc[t] is None else acc[t] + v
            for t in range(tt):
                store(l, t, i, acc[t])
            return carry

        lax.fori_loop(0, COLS, column, 0)


DWR = 304
DKR = 64
DKT = LT * DKR // 16


def block_kernel(width, nf, sc, mir, k_ref, gain_ref, mask_ref, mf_ref, win_any, wout_any, f_any, bk_any, *refs):
    halos, folds = refs[:4], refs[4 : 4 + nf]
    out_ref, gc_ref, g1_ref, g2_ref, q1_ref, q2_ref, dw_ref, dgain_ref = refs[4 + nf : 12 + nf]
    ks, buf, ext, conv, normed, act, gp, res, rows, cm, win_ref, wout_ref, f_ref, bk_ref, sem = refs[12 + nf :]
    late = [
        pltpu.make_async_copy(src, dst, sem.at[n])
        for n, (src, dst) in enumerate(((win_any, win_ref), (wout_any, wout_ref), (bk_any, bk_ref), (f_any, f_ref)))
    ]
    for copy in late:
        copy.start()
    cells = mf_ref.shape[1]
    tt = cells // 64
    hidden = win_ref.shape[1]
    extend_all(sc, mir, ext, buf, mf_ref, halos, folds)

    tap_rows(k_ref, ks, width)

    def put(l, t, i, v):
        conv[pl.ds(pl.multiple_of(t * 64 + i * 8, 8), 8), 128 * l : 128 * (l + 1)] = v

    correlate(ext, ks, tt, False, put)
    for copy in late:
        copy.wait()
    size = 256
    gain = gain_ref[...]
    valid = (lax.broadcasted_iota(jnp.int32, (1, CP), 1) < width).astype(F32)
    dgain_ref[...] = jnp.zeros_like(dgain_ref)
    inv = 1.0 / width
    coeff = 0.7978845608028654
    nt = (((1,), (1,)), ((), ()))

    def chunk(n, carry):
        at = pl.ds(pl.multiple_of(n * size, size), size)
        x = conv[at, :]
        mean = jnp.sum(x, axis=-1, keepdims=True) * inv
        cen = (x - mean) * valid
        var = jnp.sum(cen * cen, axis=-1, keepdims=True) * inv
        rstd = lax.rsqrt(var + 1e-06)
        nhat = cen * rstd
        nb = (nhat * gain).astype(BF16)
        normed[at, :] = nb
        back = bk_ref[at, :]
        for h in range(0, hidden, HB):
            v = jnp.dot(nb, win_ref[:, h : h + HB], preferred_element_type=F32)
            g = jnp.dot(back, wout_ref[:, h : h + HB], preferred_element_type=F32)
            v2 = v * v
            half = 0.5 + 0.5 * jnp.tanh(v * (coeff + (coeff * 0.044715) * v2))
            a = v * half
            slope = half + a * (1.0 - half) * (2.0 * coeff + (2.0 * coeff * 0.134145) * v2)
            act[at, h : h + HB] = a.astype(BF16)
            gp[at, h : h + HB] = (g * slope).astype(BF16)
        mixed = lax.dot_general(act[at, :], wout_ref[...], nt, preferred_element_type=F32)
        gn = lax.dot_general(gp[at, :], win_ref[...], nt, preferred_element_type=F32)
        for l in range(LT):
            res[l, at, :] = mixed[:, 128 * l : 128 * (l + 1)]
        dgain_ref[...] += jnp.broadcast_to(jnp.sum(gn * nhat, axis=0, keepdims=True), dgain_ref.shape)
        s = gn * gain
        m1 = jnp.sum(s, axis=-1, keepdims=True) * inv
        m2 = jnp.sum(s * nhat, axis=-1, keepdims=True) * inv
        gc = (rstd * (s - m1 - nhat * m2) * valid).astype(BF16).astype(F32)
        for l in range(LT):
            gc_ref[l, at, :] = gc[:, 128 * l : 128 * (l + 1)]
        return carry

    lax.fori_loop(0, cells // size, chunk, 0)
    row_messages(sc, gc_ref, rows, g1_ref, g2_ref)
    strip_messages(sc, gc_ref, q1_ref, q2_ref)
    tiles = (hidden // 128) * (DWR // 16)
    for m, (left, right) in enumerate(((normed, gp), (bk_ref, act))):
        for h in range(0, hidden, HB):
            d = lax.dot_general(
                left[...], right[:, h : h + HB], (((0,), (0,)), ((), ())), preferred_element_type=F32
            ).astype(BF16)
            for u in range(HB // 128):
                first = m * tiles + (h // 128 + u) * (DWR // 16)
                for r in range(DWR // 16):
                    dw_ref[first + r] = d[16 * r : 16 * r + 16, 128 * u : 128 * u + 128]
    dw_ref[2 * tiles :] = jnp.zeros((dw_ref.shape[0] - 2 * tiles, 16, 128), BF16)
    to_channels(res, cm)
    mixed = cm[: width * 8, :].reshape(width, 8, 128)
    out_ref[...] = (mask_ref[...].astype(F32)[None] * (f_ref[...].astype(F32) + mixed)).astype(BF16)


def taps_kernel(nf, sc, mir, x_ref, gc_ref, dgain_ref, *refs):
    halos, folds = refs[:4], refs[4 : 4 + nf]
    tiles, buf, ext, part, rows = refs[4 + nf :]
    tt = gc_ref.shape[1] // 64
    extend_all(sc, mir, ext, buf, x_ref, halos, folds)
    for l in range(LT):

        def tap_column(b, carry, l=l):
            acc = [[None, None] for _ in range(7)]
            for i in range(COLS):
                g = [gc_ref[l, t * 64 + i * 8 : t * 64 + i * 8 + 8, :] for t in range(tt)]
                for u in range(tt + 6):
                    e = ext[l, pl.ds(pl.multiple_of((u * QC + i + b) * 8, 8), 8), :]
                    for a in range(7):
                        t = u - a
                        if 0 <= t < tt:
                            v = g[t] * e
                            acc[a][u % 2] = v if acc[a][u % 2] is None else acc[a][u % 2] + v
            for a in range(7):
                part[l, pl.ds(pl.multiple_of((7 * a + b) * 8, 8), 8), :] = acc[a][0] + acc[a][1]
            return carry

        lax.fori_loop(0, 7, tap_column, 0)
    rows[...] = jnp.zeros_like(rows)
    for l in range(LT):
        for k in range(49):
            rows[l, k : k + 1, :] = jnp.sum(part[l, 8 * k : 8 * k + 8, :], axis=0, keepdims=True)
        rows[l, 49:50, :] = dgain_ref[0:1, 128 * l : 128 * (l + 1)]
        for r in range(DKR // 16):
            tiles[l * (DKR // 16) + r] = rows[l, 16 * r : 16 * r + 16, :].astype(BF16)


def field_kernel(width, nf, sc, mir, k_ref, mask_ref, c_ref, gc_ref, *refs):
    halos, folds = refs[:4], refs[4 : 4 + nf]
    out_ref, ks, buf, ext, ghost, dm, cm = refs[4 + nf :]
    cells = gc_ref.shape[1]
    tt = cells // 64
    extend(sc, ext, gc_ref, *halos)
    tap_rows(k_ref, ks, width)

    def put(l, t, i, v):
        dm[l, pl.ds(pl.multiple_of(t * 64 + i * 8, 8), 8), :] = v

    correlate(ext, ks, tt, True, put)

    @pl.when(sc[IS_TOP] == 1)
    def _():
        ghost[...] = jnp.zeros_like(ghost)
        fold_rows(sc, mir, folds, buf, ghost, 0)
        for l in range(LT):

            def column(i, carry, l=l):
                for k in range(3):
                    at = pl.ds(pl.multiple_of((tt - 1 - k) * 64 + i * 8, 8), 8)
                    acc = dm[l, at, :]
                    for r in range(3 - k):
                        for b in range(7):
                            tap = 7 * (4 + k + r) + b
                            e = ghost[l, pl.ds(pl.multiple_of((r * QC + i + b) * 8, 8), 8), :]
                            acc = acc + jnp.broadcast_to(ks[l, tap : tap + 1, :], (8, 128)) * e
                    dm[l, at, :] = acc
                return carry

            lax.fori_loop(0, COLS, column, 0)

    to_channels(dm, cm)
    total = cm[: width * 8, :].reshape(width, 8, 128)
    out_ref[...] = (mask_ref[...].astype(F32)[None] * (c_ref[...].astype(F32) + total)).astype(BF16)


def unpack_kernel(width, hidden, factor, per, half, sc, own_ref, got_ref, gin_ref, gout_ref, gk_ref, gg_ref):
    blocks = (hidden + 127) // 128
    blocks += blocks % 2
    tr = DWR // 16

    for core in range(2):

        @pl.when(sc[CORE] == core)
        def _(core=core):
            def tile(n):
                ref = own_ref if n // half == core else got_ref
                chunk = lax.bitwise_xor(jnp.int32((n % half) // per), sc[ME])
                return ref[chunk * per + n % per].astype(F32) * factor

            for m, out in enumerate((gin_ref, gout_ref)):
                for cb in range(blocks):
                    w = min(128, hidden - 128 * cb)
                    if w <= 0:
                        continue
                    for r in range(tr):
                        rows = min(16, width - 16 * r)
                        out[16 * r : 16 * r + rows, 128 * cb : 128 * cb + w] = tile((m * blocks + cb) * tr + r)[:rows, :w]

    for l in range(LT):
        w = lanes(l, width)
        for r in range(DKR // 16):
            n = half + l * (DKR // 16) + r
            v = (own_ref[n].astype(F32) + got_ref[n].astype(F32)) * factor
            rows = min(16, 49 - 16 * r)
            gk_ref[16 * r : 16 * r + rows, 128 * l : 128 * l + w] = v[:rows, :w]
            if rows < 16:
                gg_ref[:, 128 * l : 128 * l + w] = v[rows : rows + 1, :w]


def swaps(n_lat, n_lon, bits):
    ml, mo = bits
    return [(l * n_lon + o, (l ^ ml) * n_lon + (o ^ mo)) for l in range(n_lat) for o in range(n_lon)]


def lat_swaps(n_lat, n_lon):
    first = [(l * n_lon + o, (l ^ 1) * n_lon + o) for l in range(n_lat) for o in range(n_lon)]
    second = []
    for l in range(n_lat):
        for o in range(n_lon):
            if l == n_lat - 1:
                second.append((l * n_lon + o, l * n_lon + (o ^ 1)))
            elif l > 0:
                other = l + 1 if l % 2 else l - 1
                second.append((l * n_lon + o, other * n_lon + o))
    return first, second


def lon_swaps(n_lat, n_lon):
    first = [(l * n_lon + o, l * n_lon + (o ^ 1)) for l in range(n_lat) for o in range(n_lon)]
    second = []
    for l in range(n_lat):
        for o in range(n_lon):
            other = (o + 1) % n_lon if o % 2 else (o - 1) % n_lon
            second.append((l * n_lon + o, l * n_lon + other))
    return first, second


def fold_gather(own, pair, n_lat, n_lon):
    units = [jnp.stack([own, pair])]
    top = n_lat - 1
    bit = 2
    while bit < n_lon:
        have = jnp.concatenate(units) if len(units) > 1 else units[0]
        end = min(4 * bit, n_lon)
        for d in range(bit, end, bit):
            pairs = [(top * n_lon + o, top * n_lon + (o ^ d)) for o in range(n_lon)]
            units.append(lax.ppermute(have, AXES, pairs))
        bit = end
    return units


def stages(n_lat, n_lon):
    out = [[(1, 0)]]
    rest = [(1 << b, 0) for b in range(1, n_lat.bit_length() - 1)] + [(0, 1 << b) for b in range(n_lon.bit_length() - 1)]
    while rest:
        out.append(rest[:2])
        rest = rest[2:]
    return out


def group_index(group, lat, lon):
    value = jnp.int32(0)
    for ml, mo in group:
        bit = (lat & ml) != 0 if ml else (lon & mo) != 0
        value = 2 * value + bit.astype(jnp.int32)
    return value


def group_masks(group):
    masks = []
    for d in range(1 << len(group)):
        ml = mo = 0
        for k, (gl, go) in enumerate(group):
            if d >> (len(group) - 1 - k) & 1:
                ml, mo = ml | gl, mo | go
        masks.append((ml, mo))
    return masks


def scatter_stage(x, group, lat, lon, n_lat, n_lon, beside=None):
    n = 1 << len(group)
    x = x.reshape((n, x.shape[0] // n) + x.shape[1:])
    idx = group_index(group, lat, lon)
    masks = group_masks(group)
    got = []
    for d in range(1, n):
        piece = lax.dynamic_index_in_dim(x, idx ^ d, 0, False)
        got.append(lax.ppermute(piece, AXES, swaps(n_lat, n_lon, masks[d])))
    if beside is not None:
        got, beside = lax.optimization_barrier((got, beside))
    total = lax.dynamic_index_in_dim(x, idx, 0, False).astype(F32)
    for g in got:
        total = total + g.astype(F32)
    return total.astype(BF16), beside


def packet_kernel(*refs):
    ins, out_ref = refs[:-1], refs[-1]
    size = ins[0].shape[0] - DKT
    total = ins[0][size:].astype(F32)
    for k, ref in enumerate(ins):
        out_ref[k * size : (k + 1) * size] = ref[:size]
        if k:
            total = total + ref[size:].astype(F32)
    out_ref[len(ins) * size :] = total.astype(BF16)


def gather_stage(packet, group, n_lat, n_lon, beside=None):
    masks = group_masks(group)
    got = [lax.ppermute(packet, AXES, swaps(n_lat, n_lon, masks[d])) for d in range(1, len(masks))]
    if beside is not None:
        got, beside = lax.optimization_barrier((got, beside))
    return [packet] + got, beside


def join(pieces):
    n, size = len(pieces), pieces[0].shape[0] - DKT
    return pl.pallas_call(
        packet_kernel,
        out_shape=jax.ShapeDtypeStruct((n * size + DKT, 16, 128), BF16),
        in_specs=[VM] * n,
        out_specs=VM,
        compiler_params=params(),
        name="join",
        cost_estimate=cost(1),
    )(*pieces)


def body(field_in, sea_mask, mirror, kernel, norm_gain, proj_in, proj_out, cotangent):
    nrows, ncols, width = field_in.shape
    hidden = proj_in.shape[1]
    n_lat, n_lon = lax.axis_size("lat"), lax.axis_size("lon")
    assert ncols == COLS and nrows % 16 == 0 and n_lat % 2 == 0 and n_lon % 2 == 0
    lat, lon = lax.axis_index("lat"), lax.axis_index("lon")
    cells = nrows * ncols
    tt = nrows // SUB
    groups = stages(n_lat, n_lon)
    me = jnp.int32(0)
    for group in groups[1:]:
        me = (me << len(group)) + group_index(group, lat, lon)
    sc = jnp.stack(
        [1 - lon % 2, 1 - lat % 2, (lat == n_lat - 1).astype(jnp.int32), lon, lon * ncols, me, lat % 2, jnp.int32(0)]
    ).astype(jnp.int32)
    assert nrows == 128 and n_lon % 4 == 0
    hp = -(-hidden // HB) * HB
    win = jnp.pad(proj_in, ((0, CP - width), (0, hp - hidden)))
    wout = jnp.pad(proj_out.T, ((0, CP - width), (0, hp - hidden)))
    gain = jnp.pad(norm_gain, (0, CP - width)).reshape(1, CP)
    field_c = field_in.transpose(2, 1, 0)
    cot_c = cotangent.transpose(2, 1, 0)
    mask_c = sea_mask.T

    s = jax.ShapeDtypeStruct
    row_msg = s((3, COLS, CP), BF16)
    strip_msg = s((LT, 3 * tt * 8 + 32, 128), BF16)
    channels = pltpu.VMEM((CP * 8, 128), F32)
    cells_f32 = pltpu.VMEM((LT, cells, 128), F32)
    ext_f32 = pltpu.VMEM((LT, (tt + 6) * QC * 8, 128), F32)
    fold_f32 = pltpu.VMEM((LT, n_lon * 24, 128), F32)
    rows_f32 = pltpu.VMEM((6, COLS, CP), F32)
    taps_f32 = pltpu.VMEM((LT, 56, 128), F32)
    mf, p1, p2, q1, q2 = pl.pallas_call(
        prepare_kernel,
        out_shape=(s((LT, cells, 128), F32), row_msg, row_msg, strip_msg, strip_msg),
        in_specs=[SM, VM, VM],
        out_specs=(VM,) * 5,
        scratch_shapes=[channels, rows_f32],
        compiler_params=params(),
        name="prepare",
        cost_estimate=cost(3),
    )(sc, mask_c, field_c)
    bk = pl.pallas_call(
        back_kernel,
        out_shape=s((cells, CP), BF16),
        in_specs=[VM, VM],
        out_specs=VM,
        scratch_shapes=[channels, cells_f32],
        compiler_params=params(),
        name="back",
        cost_estimate=cost(3),
    )(mask_c, cot_c)

    lat1, lat2 = lat_swaps(n_lat, n_lon)
    lon1, lon2 = lon_swaps(n_lat, n_lon)

    def halo(q1, q2, p1, p2, beside):
        r1 = lax.ppermute(p1, AXES, lat1)
        r2 = lax.ppermute(p2, AXES, lat2)
        r1, r2, beside = lax.optimization_barrier((r1, r2, beside))
        q1, q2 = pl.pallas_call(
            corners_kernel,
            out_shape=(strip_msg, strip_msg),
            in_specs=[SM, VM, VM, ANY, ANY],
            out_specs=(ANY, ANY),
            scratch_shapes=[
                pltpu.VMEM((LT, 64, 128), F32),
                pltpu.VMEM((2, LT, 32, 128), BF16),
                pltpu.SemaphoreType.DMA((2,)),
            ],
            input_output_aliases={3: 0, 4: 1},
            compiler_params=params(),
            name="corners",
            cost_estimate=cost(1),
        )(sc, r1, r2, q1, q2)
        s1 = lax.ppermute(q1, AXES, lon1)
        s2 = lax.ppermute(q2, AXES, lon2)
        return [s1, s2, r1, r2] + fold_gather(p2, r2, n_lat, n_lon), beside

    halos, bk = halo(q1, q2, p1, p2, bk)
    nf = len(halos) - 4
    count = 2 * (hp // 128) * (DWR // 16)
    devices = n_lat * n_lon
    per = -(-count // devices)
    half = per * devices // 2
    out, gc, g1, g2, q1, q2, dw, dgain = pl.pallas_call(
        lambda *refs: block_kernel(width, nf, *refs),
        out_shape=(
            s((width, COLS, nrows), BF16),
            s((LT, cells, 128), F32),
            row_msg,
            row_msg,
            strip_msg,
            strip_msg,
            s((per * devices, 16, 128), BF16),
            s((8, CP), F32),
        ),
        in_specs=[SM, SM] + [VM] * 4 + [ANY] * 4 + [VM] * len(halos),
        out_specs=(VM,) * 8,
        scratch_shapes=[
            taps_f32,
            fold_f32,
            ext_f32,
            pltpu.VMEM((cells, CP), F32),
            pltpu.VMEM((cells, CP), BF16),
            pltpu.VMEM((cells, hp), BF16),
            pltpu.VMEM((cells, hp), BF16),
            cells_f32,
            rows_f32,
            channels,
            pltpu.VMEM((CP, hp), BF16),
            pltpu.VMEM((CP, hp), BF16),
            pltpu.VMEM((width, COLS, nrows), BF16),
            pltpu.VMEM((cells, CP), BF16),
            pltpu.SemaphoreType.DMA((4,)),
        ],
        compiler_params=params(),
        name="block",
        cost_estimate=cost(18),
    )(sc, mirror, kernel, gain, mask_c, mf, win, wout, field_c, bk, *halos)

    first, _ = scatter_stage(dw, groups[0], lat, lon, n_lat, n_lon)
    ghalos, first = halo(q1, q2, g1, g2, first)
    gc_taps, dgain, _ = lax.optimization_barrier((gc, dgain, first))
    dk = pl.pallas_call(
        lambda *refs: taps_kernel(nf, *refs),
        out_shape=s((LT * DKR // 16, 16, 128), BF16),
        in_specs=[SM, SM] + [VM] * (len(halos) + 3),
        out_specs=VM,
        scratch_shapes=[fold_f32, ext_f32, pltpu.VMEM((LT, 49 * 8, 128), F32), pltpu.VMEM((LT, DKR, 128), F32)],
        compiler_params=params(),
        name="taps",
        cost_estimate=cost(1),
    )(sc, mirror, mf, gc_taps, dgain, *halos)
    x = first
    for k, group in enumerate(groups[1:]):
        beside = (dk, ghalos) if k == 0 else None
        x, beside = scatter_stage(x, group, lat, lon, n_lat, n_lon, beside)
        if beside is not None:
            dk, ghalos = beside
    grad_field = pl.pallas_call(
        lambda *refs: field_kernel(width, nf, *refs),
        out_shape=s((width, COLS, nrows), BF16),
        in_specs=[SM, SM] + [VM] * (len(ghalos) + 4),
        out_specs=VM,
        scratch_shapes=[taps_f32, fold_f32, ext_f32, pltpu.VMEM((LT, 3 * QC * 8, 128), F32), cells_f32, channels],
        compiler_params=params(),
        name="field",
        cost_estimate=cost(10),
    )(sc, mirror, kernel, mask_c, cot_c, gc, *ghalos)
    packet = jnp.concatenate([x, dk], axis=0)
    for group in reversed(groups[1:]):
        beside = grad_field if group is groups[1] else None
        pieces, beside = gather_stage(packet, group, n_lat, n_lon, beside)
        grad_field = grad_field if beside is None else beside
        packet = join(pieces)
    pieces, _ = gather_stage(packet, groups[0], n_lat, n_lon)
    factor = float(1.0 / np.sqrt(np.float32(nrows * n_lat * ncols * n_lon)))
    gin, gout, gk, gg = pl.pallas_call(
        lambda *refs: unpack_kernel(width, hidden, factor, per, half, *refs),
        out_shape=(s((width, hidden), F32), s((width, hidden), F32), s((49, width), F32), s((1, width), F32)),
        in_specs=[SM, VM, VM],
        out_specs=(VM,) * 4,
        compiler_params=params(),
        name="unpack",
        cost_estimate=cost(3),
    )(sc, pieces[0], pieces[1])
    return out.transpose(2, 1, 0), grad_field.transpose(2, 1, 0), gin, gout.T, gk, gg.reshape(width)


def solution(mesh):
    in_specs = (
        P("lat", "lon", None),
        P("lat", "lon"),
        P(),
        P(),
        P(),
        P(),
        P(),
        P("lat", "lon", None),
    )
    out_specs = (P("lat", "lon", None), P("lat", "lon", None), P(), P(), P(), P())
    return jax.shard_map(body, mesh=mesh, in_specs=in_specs, out_specs=out_specs, check_vma=False)
```

```python
import jax
import jax.numpy as jnp
import numpy as np
from jax import lax
from jax.experimental import pallas as pl
from jax.experimental.pallas import tpu as pltpu
from jax.sharding import PartitionSpec as P

F32 = jnp.float32
BF16 = jnp.bfloat16
AXES = ("lat", "lon")
SUB = 8
COLS = 8
QC = COLS + 6
LT = 3
CP = LT * 128
HB = 256
VM = pl.BlockSpec(memory_space=pltpu.VMEM)
SM = pl.BlockSpec(memory_space=pltpu.SMEM)
ANY = pl.BlockSpec(memory_space=pl.ANY)

EVEN_LON, EVEN_LAT, IS_TOP, LON, START, ME, CORE = range(7)


def cost(us):
    return pl.CostEstimate(flops=int(us * 1e6), bytes_accessed=int(us * 2e6), transcendentals=0)


def params(mib=60):
    return pltpu.CompilerParams(vmem_limit_bytes=mib * 1024 * 1024)


def lanes(l, width):
    return min(128, width - 128 * l)


def tap_rows(k_ref, ks, width):
    ks[...] = jnp.zeros_like(ks)
    for l in range(LT):
        w = lanes(l, width)
        ks[l, : k_ref.shape[0], :w] = k_ref[:, 128 * l : 128 * l + w]


def to_cells(src, l, i, put):
    x = src[pl.ds(l * 1024 + i, 128, stride=8), :].T
    for s in range(SUB):
        for t in (0, 8):
            put(pl.ds(t * 64 + i * 8 + s, 8, stride=64), x[16 * s + t : 16 * s + t + 8])


def to_channels(src, dst):
    for l in range(LT):
        for i in range(COLS):
            parts = [src[l, pl.ds(t * 64 + i * 8 + s, 8, stride=64), :] for s in range(SUB) for t in (0, 8)]
            dst[pl.ds(l * 1024 + i, 128, stride=8), :] = jnp.concatenate(parts, axis=0).T


def row_messages(sc, x_ref, rows, p1_ref, p2_ref):
    tt = x_ref.shape[1] // 64
    for l in range(LT):
        for r in range(3):
            rows[r, :, 128 * l : 128 * (l + 1)] = x_ref[l, pl.ds(r * 64, 8, stride=8), :]
            rows[3 + r, :, 128 * l : 128 * (l + 1)] = x_ref[l, pl.ds((tt - 3 + r) * 64 + 7, 8, stride=8), :]
    even = sc[EVEN_LAT]
    p1_ref[...] = rows[pl.ds(3 * even, 3)].astype(BF16)
    p2_ref[...] = rows[pl.ds(3 - 3 * even, 3)].astype(BF16)


def strip_messages(sc, x_ref, q1_ref, q2_ref):
    tt = x_ref.shape[1] // 64
    even = sc[EVEN_LON]
    for q_ref, first in ((q1_ref, 5 * even), (q2_ref, 5 - 5 * even)):
        for l in range(LT):
            for c in range(3):
                for t in range(0, tt, 2):
                    a = x_ref[l, pl.ds(pl.multiple_of(t * 64 + (first + c) * 8, 8), 8), :]
                    b = x_ref[l, pl.ds(pl.multiple_of(t * 64 + 64 + (first + c) * 8, 8), 8), :]
                    q_ref[l, (c * tt + t) * 8 : (c * tt + t) * 8 + 16, :] = jnp.concatenate([a, b], 0).astype(BF16)
            q_ref[l, 3 * tt * 8 :, :] = jnp.zeros((32, 128), BF16)


def corners_kernel(sc, p1_ref, p2_ref, _, __, q1_ref, q2_ref, lu, corner, sem):
    even_lat, even = sc[EVEN_LAT], sc[EVEN_LON]
    p1, p2 = p1_ref[...].astype(F32), p2_ref[...].astype(F32)
    lower = jnp.where(even_lat == 1, p2, p1)
    upper = jnp.where(even_lat == 1, p1, p2)
    for l in range(LT):
        for r in range(3):
            lu[l, 8 * r : 8 * r + 8, :] = lower[r, :, 128 * l : 128 * (l + 1)]
            lu[l, 24 + 8 * r : 32 + 8 * r, :] = upper[r, :, 128 * l : 128 * (l + 1)]
        lu[l, 48:, :] = jnp.zeros((16, 128), F32)
    copies = []
    for n, (q_ref, first) in enumerate(((q1_ref, 5 * even), (q2_ref, 5 - 5 * even))):
        for l in range(LT):
            k = [lu[l, pl.ds(first + c, 8, stride=8), :] for c in range(3)]
            k.append(jnp.zeros((8, 128), F32))
            corner[n, l] = jnp.concatenate(k, 0).astype(BF16)
        rows = q_ref.shape[1]
        copies.append(pltpu.make_async_copy(corner.at[n], q_ref.at[:, pl.ds(rows - 32, 32), :], sem.at[n]))
        copies[-1].start()
    for copy in copies:
        copy.wait()


def masked_cells(mask_ref, src, cm, dst):
    width = src.shape[0]
    m = mask_ref[...].astype(F32)[None]
    cm[width * 8 :, :] = jnp.zeros((cm.shape[0] - width * 8, 128), F32)
    cm[: width * 8, :] = (src[...].astype(F32) * m).reshape(width * 8, 128)
    for l in range(LT):
        for i in range(COLS):

            def put(at, v, l=l):
                dst[l, at, :] = v

            to_cells(cm, l, i, put)


def prepare_kernel(sc, mask_ref, f_ref, mf_ref, p1_ref, p2_ref, q1_ref, q2_ref, cm, rows):
    masked_cells(mask_ref, f_ref, cm, mf_ref)
    row_messages(sc, mf_ref, rows, p1_ref, p2_ref)
    strip_messages(sc, mf_ref, q1_ref, q2_ref)


def back_kernel(mask_ref, c_ref, bk_ref, cm, ct):
    masked_cells(mask_ref, c_ref, cm, ct)
    for l in range(LT):
        bk_ref[:, 128 * l : 128 * (l + 1)] = ct[l].astype(BF16)


def extend(sc, ext, x_ref, q1_ref, q2_ref, p1_ref, p2_ref):
    tt = x_ref.shape[1] // 64
    even_lat, even_lon, top = sc[EVEN_LAT], sc[EVEN_LON], sc[IS_TOP]
    for l in range(LT):
        for t in range(tt):
            ext[l, ((t + 3) * QC + 3) * 8 : ((t + 3) * QC + 3) * 8 + 64, :] = x_ref[l, t * 64 : t * 64 + 64, :]
    sides = ((q1_ref, even_lon), (q2_ref, 1 - even_lon))
    for q_ref, right in sides:
        for l in range(LT):
            for c in range(3):
                for t in range(0, tt, 2):
                    v = q_ref[l, (c * tt + t) * 8 : (c * tt + t) * 8 + 16, :].astype(F32)
                    for u in range(2):
                        at = ((t + u + 3) * QC + 11 * right + c) * 8
                        ext[l, pl.ds(pl.multiple_of(at, 8), 8), :] = v[8 * u : 8 * u + 8]
    for l in range(LT):
        for r in range(3):
            for q in range(QC):
                lo = ext[l, ((tt + r) * QC + q) * 8 : ((tt + r) * QC + q) * 8 + 8, :]
                ext[l, (r * QC + q) * 8 : (r * QC + q) * 8 + 8, :] = pltpu.roll(lo, 1, 0)
                hi = ext[l, ((3 + r) * QC + q) * 8 : ((3 + r) * QC + q) * 8 + 8, :]
                at = ((tt + 3 + r) * QC + q) * 8
                ext[l, at : at + 8, :] = pltpu.roll(hi, 7, 0)
    keep = (1 - top).astype(F32)
    p1, p2 = p1_ref[...].astype(F32), p2_ref[...].astype(F32)
    lower = jnp.where(even_lat == 1, p2, p1)
    upper = jnp.where(even_lat == 1, p1, p2) * keep
    for l in range(LT):
        for r in range(3):
            ext[l, pl.ds((r * QC + 3) * 8, 8, stride=8), :] = lower[r, :, 128 * l : 128 * (l + 1)]
            ext[l, pl.ds(((tt + 3 + r) * QC + 3) * 8 + 7, 8, stride=8), :] = upper[r, :, 128 * l : 128 * (l + 1)]
    for q_ref, right in sides:
        first = 11 * right
        for l in range(LT):
            corner = q_ref[l, 3 * tt * 8 : 3 * tt * 8 + 32, :].astype(F32)
            for c in range(3):
                for r in range(3):
                    ext[l, pl.ds((r * QC + first + c) * 8, 1), :] = corner[8 * c + r : 8 * c + r + 1]
                    at = ((tt + 3 + r) * QC + first + c) * 8 + 7
                    ext[l, pl.ds(at, 1), :] = corner[8 * c + 3 + r : 8 * c + 4 + r] * keep


def fold_rows(sc, mir, fold_refs, buf, dst, base):
    first = 0
    for ref in fold_refs:
        for u in range(ref.shape[0]):
            for r in range(3):
                at = ((first + u) * 3 + r) * 8
                v = ref[u, r].astype(F32)
                for l in range(LT):
                    buf[l, at : at + 8, :] = v[:, 128 * l : 128 * (l + 1)]
        first += ref.shape[0]
    total = mir.shape[0]
    for q in range(QC):
        col = sc[START] - 3 + q
        col = jnp.where(col < 0, col + total, col)
        col = jnp.where(col >= total, col - total, col)
        m = mir[col]
        unit = lax.bitwise_xor(lax.shift_right_logical(m, 3), sc[LON])
        at = unit * 24 + lax.bitwise_and(m, 7)
        for k in range(3):
            for l in range(LT):
                dst[l, pl.ds(base + (k * QC + q) * 8 + 7, 1), :] = buf[l, pl.ds(at + (2 - k) * 8, 1), :]


def extend_all(sc, mir, ext, buf, x_ref, halos, folds):
    extend(sc, ext, x_ref, *halos)

    @pl.when(sc[IS_TOP] == 1)
    def _():
        fold_rows(sc, mir, folds, buf, ext, (x_ref.shape[1] // 64 + 3) * QC * 8)


def correlate(ext, ks, tt, flip, store):
    for l in range(LT):

        def column(i, carry, l=l):
            acc = [None] * tt
            for b in range(7):
                k = []
                for a in range(7):
                    tap = 7 * a + b
                    tap = 48 - tap if flip else tap
                    k.append(jnp.broadcast_to(ks[l, tap : tap + 1, :], (8, 128)))
                for u in range(tt + 6):
                    e = ext[l, pl.ds(pl.multiple_of((u * QC + i + b) * 8, 8), 8), :]
                    for a in range(7):
                        t = u - a
                        if 0 <= t < tt:
                            v = k[a] * e
                            acc[t] = v if acc[t] is None else acc[t] + v
            for t in range(tt):
                store(l, t, i, acc[t])
            return carry

        lax.fori_loop(0, COLS, column, 0)


DWR = 304
DKR = 64
DKT = LT * DKR // 16


def block_kernel(width, nf, sc, mir, k_ref, gain_ref, mask_ref, mf_ref, win_any, wout_any, f_any, bk_any, *refs):
    halos, folds = refs[:4], refs[4 : 4 + nf]
    out_ref, gc_ref, g1_ref, g2_ref, q1_ref, q2_ref, dw_ref, dgain_ref = refs[4 + nf : 12 + nf]
    ks, buf, ext, conv, normed, act, gp, res, rows, cm, win_ref, wout_ref, f_ref, bk_ref, sem = refs[12 + nf :]
    late = [
        pltpu.make_async_copy(src, dst, sem.at[n])
        for n, (src, dst) in enumerate(((win_any, win_ref), (wout_any, wout_ref), (bk_any, bk_ref), (f_any, f_ref)))
    ]
    for copy in late:
        copy.start()
    cells = mf_ref.shape[1]
    tt = cells // 64
    hidden = win_ref.shape[1]
    extend_all(sc, mir, ext, buf, mf_ref, halos, folds)

    tap_rows(k_ref, ks, width)

    def put(l, t, i, v):
        conv[pl.ds(pl.multiple_of(t * 64 + i * 8, 8), 8), 128 * l : 128 * (l + 1)] = v

    correlate(ext, ks, tt, False, put)
    for copy in late:
        copy.wait()
    size = 256
    gain = gain_ref[...]
    valid = (lax.broadcasted_iota(jnp.int32, (1, CP), 1) < width).astype(F32)
    dgain_ref[...] = jnp.zeros_like(dgain_ref)
    inv = 1.0 / width
    coeff = 0.7978845608028654
    nt = (((1,), (1,)), ((), ()))

    def chunk(n, carry):
        at = pl.ds(pl.multiple_of(n * size, size), size)
        x = conv[at, :]
        mean = jnp.sum(x, axis=-1, keepdims=True) * inv
        cen = (x - mean) * valid
        var = jnp.sum(cen * cen, axis=-1, keepdims=True) * inv
        rstd = lax.rsqrt(var + 1e-06)
        nhat = cen * rstd
        nb = (nhat * gain).astype(BF16)
        normed[at, :] = nb
        back = bk_ref[at, :]
        for h in range(0, hidden, HB):
            v = jnp.dot(nb, win_ref[:, h : h + HB], preferred_element_type=F32)
            g = jnp.dot(back, wout_ref[:, h : h + HB], preferred_element_type=F32)
            v2 = v * v
            half = 0.5 + 0.5 * jnp.tanh(v * (coeff + (coeff * 0.044715) * v2))
            a = v * half
            slope = half + a * (1.0 - half) * (2.0 * coeff + (2.0 * coeff * 0.134145) * v2)
            act[at, h : h + HB] = a.astype(BF16)
            gp[at, h : h + HB] = (g * slope).astype(BF16)
        mixed = lax.dot_general(act[at, :], wout_ref[...], nt, preferred_element_type=F32)
        gn = lax.dot_general(gp[at, :], win_ref[...], nt, preferred_element_type=F32)
        for l in range(LT):
            res[l, at, :] = mixed[:, 128 * l : 128 * (l + 1)]
        dgain_ref[...] += jnp.broadcast_to(jnp.sum(gn * nhat, axis=0, keepdims=True), dgain_ref.shape)
        s = gn * gain
        m1 = jnp.sum(s, axis=-1, keepdims=True) * inv
        m2 = jnp.sum(s * nhat, axis=-1, keepdims=True) * inv
        gc = (rstd * (s - m1 - nhat * m2) * valid).astype(BF16).astype(F32)
        for l in range(LT):
            gc_ref[l, at, :] = gc[:, 128 * l : 128 * (l + 1)]
        return carry

    lax.fori_loop(0, cells // size, chunk, 0)
    row_messages(sc, gc_ref, rows, g1_ref, g2_ref)
    strip_messages(sc, gc_ref, q1_ref, q2_ref)
    tiles = (hidden // 128) * (DWR // 16)
    for m, (left, right) in enumerate(((normed, gp), (bk_ref, act))):
        for h in range(0, hidden, HB):
            d = lax.dot_general(
                left[...], right[:, h : h + HB], (((0,), (0,)), ((), ())), preferred_element_type=F32
            ).astype(BF16)
            for u in range(HB // 128):
                first = m * tiles + (h // 128 + u) * (DWR // 16)
                for r in range(DWR // 16):
                    dw_ref[first + r] = d[16 * r : 16 * r + 16, 128 * u : 128 * u + 128]
    dw_ref[2 * tiles :] = jnp.zeros((dw_ref.shape[0] - 2 * tiles, 16, 128), BF16)
    to_channels(res, cm)
    mixed = cm[: width * 8, :].reshape(width, 8, 128)
    out_ref[...] = (mask_ref[...].astype(F32)[None] * (f_ref[...].astype(F32) + mixed)).astype(BF16)


def taps_kernel(nf, sc, mir, x_ref, gc_ref, dgain_ref, *refs):
    halos, folds = refs[:4], refs[4 : 4 + nf]
    tiles, buf, ext, part, rows = refs[4 + nf :]
    tt = gc_ref.shape[1] // 64
    extend_all(sc, mir, ext, buf, x_ref, halos, folds)
    for l in range(LT):

        def tap_column(b, carry, l=l):
            acc = [[None, None] for _ in range(7)]
            for i in range(COLS):
                g = [gc_ref[l, t * 64 + i * 8 : t * 64 + i * 8 + 8, :] for t in range(tt)]
                for u in range(tt + 6):
                    e = ext[l, pl.ds(pl.multiple_of((u * QC + i + b) * 8, 8), 8), :]
                    for a in range(7):
                        t = u - a
                        if 0 <= t < tt:
                            v = g[t] * e
                            acc[a][u % 2] = v if acc[a][u % 2] is None else acc[a][u % 2] + v
            for a in range(7):
                part[l, pl.ds(pl.multiple_of((7 * a + b) * 8, 8), 8), :] = acc[a][0] + acc[a][1]
            return carry

        lax.fori_loop(0, 7, tap_column, 0)
    rows[...] = jnp.zeros_like(rows)
    for l in range(LT):
        for k in range(49):
            rows[l, k : k + 1, :] = jnp.sum(part[l, 8 * k : 8 * k + 8, :], axis=0, keepdims=True)
        rows[l, 49:50, :] = dgain_ref[0:1, 128 * l : 128 * (l + 1)]
        for r in range(DKR // 16):
            tiles[l * (DKR // 16) + r] = rows[l, 16 * r : 16 * r + 16, :].astype(BF16)


def field_kernel(width, nf, sc, mir, k_ref, mask_ref, c_ref, gc_ref, *refs):
    halos, folds = refs[:4], refs[4 : 4 + nf]
    out_ref, ks, buf, ext, ghost, dm, cm = refs[4 + nf :]
    cells = gc_ref.shape[1]
    tt = cells // 64
    extend(sc, ext, gc_ref, *halos)
    tap_rows(k_ref, ks, width)

    def put(l, t, i, v):
        dm[l, pl.ds(pl.multiple_of(t * 64 + i * 8, 8), 8), :] = v

    correlate(ext, ks, tt, True, put)

    @pl.when(sc[IS_TOP] == 1)
    def _():
        ghost[...] = jnp.zeros_like(ghost)
        fold_rows(sc, mir, folds, buf, ghost, 0)
        for l in range(LT):

            def column(i, carry, l=l):
                for k in range(3):
                    at = pl.ds(pl.multiple_of((tt - 1 - k) * 64 + i * 8, 8), 8)
                    acc = dm[l, at, :]
                    for r in range(3 - k):
                        for b in range(7):
                            tap = 7 * (4 + k + r) + b
                            e = ghost[l, pl.ds(pl.multiple_of((r * QC + i + b) * 8, 8), 8), :]
                            acc = acc + jnp.broadcast_to(ks[l, tap : tap + 1, :], (8, 128)) * e
                    dm[l, at, :] = acc
                return carry

            lax.fori_loop(0, COLS, column, 0)

    to_channels(dm, cm)
    total = cm[: width * 8, :].reshape(width, 8, 128)
    out_ref[...] = (mask_ref[...].astype(F32)[None] * (c_ref[...].astype(F32) + total)).astype(BF16)


def unpack_kernel(width, hidden, factor, per, half, sc, own_ref, got_ref, gin_ref, gout_ref, gk_ref, gg_ref):
    blocks = (hidden + 127) // 128
    blocks += blocks % 2
    tr = DWR // 16

    for core in range(2):

        @pl.when(sc[CORE] == core)
        def _(core=core):
            def tile(n):
                ref = own_ref if n // half == core else got_ref
                chunk = lax.bitwise_xor(jnp.int32((n % half) // per), sc[ME])
                return ref[chunk * per + n % per].astype(F32) * factor

            for m, out in enumerate((gin_ref, gout_ref)):
                for cb in range(blocks):
                    w = min(128, hidden - 128 * cb)
                    if w <= 0:
                        continue
                    for r in range(tr):
                        rows = min(16, width - 16 * r)
                        out[16 * r : 16 * r + rows, 128 * cb : 128 * cb + w] = tile((m * blocks + cb) * tr + r)[:rows, :w]

    for l in range(LT):
        w = lanes(l, width)
        for r in range(DKR // 16):
            n = half + l * (DKR // 16) + r
            v = (own_ref[n].astype(F32) + got_ref[n].astype(F32)) * factor
            rows = min(16, 49 - 16 * r)
            gk_ref[16 * r : 16 * r + rows, 128 * l : 128 * l + w] = v[:rows, :w]
            if rows < 16:
                gg_ref[128 * l : 128 * l + w] = v[rows, :w]


def swaps(n_lat, n_lon, bits):
    ml, mo = bits
    return [(l * n_lon + o, (l ^ ml) * n_lon + (o ^ mo)) for l in range(n_lat) for o in range(n_lon)]


def lat_swaps(n_lat, n_lon):
    first = [(l * n_lon + o, (l ^ 1) * n_lon + o) for l in range(n_lat) for o in range(n_lon)]
    second = []
    for l in range(n_lat):
        for o in range(n_lon):
            if l == n_lat - 1:
                second.append((l * n_lon + o, l * n_lon + (o ^ 1)))
            elif l > 0:
                other = l + 1 if l % 2 else l - 1
                second.append((l * n_lon + o, other * n_lon + o))
    return first, second


def lon_swaps(n_lat, n_lon):
    first = [(l * n_lon + o, l * n_lon + (o ^ 1)) for l in range(n_lat) for o in range(n_lon)]
    second = []
    for l in range(n_lat):
        for o in range(n_lon):
            other = (o + 1) % n_lon if o % 2 else (o - 1) % n_lon
            second.append((l * n_lon + o, l * n_lon + other))
    return first, second


def fold_gather(own, pair, n_lat, n_lon):
    units = [jnp.stack([own, pair])]
    top = n_lat - 1
    bit = 2
    while bit < n_lon:
        have = jnp.concatenate(units) if len(units) > 1 else units[0]
        end = min(4 * bit, n_lon)
        for d in range(bit, end, bit):
            pairs = [(top * n_lon + o, top * n_lon + (o ^ d)) for o in range(n_lon)]
            units.append(lax.ppermute(have, AXES, pairs))
        bit = end
    return units


def stages(n_lat, n_lon):
    out = [[(1, 0)]]
    rest = [(1 << b, 0) for b in range(1, n_lat.bit_length() - 1)] + [(0, 1 << b) for b in range(n_lon.bit_length() - 1)]
    while rest:
        out.append(rest[:2])
        rest = rest[2:]
    return out


def group_index(group, lat, lon):
    value = jnp.int32(0)
    for ml, mo in group:
        bit = (lat & ml) != 0 if ml else (lon & mo) != 0
        value = 2 * value + bit.astype(jnp.int32)
    return value


def group_masks(group):
    masks = []
    for d in range(1 << len(group)):
        ml = mo = 0
        for k, (gl, go) in enumerate(group):
            if d >> (len(group) - 1 - k) & 1:
                ml, mo = ml | gl, mo | go
        masks.append((ml, mo))
    return masks


def scatter_stage(x, group, lat, lon, n_lat, n_lon, beside=None):
    n = 1 << len(group)
    x = x.reshape((n, x.shape[0] // n) + x.shape[1:])
    idx = group_index(group, lat, lon)
    masks = group_masks(group)
    got = []
    for d in range(1, n):
        piece = lax.dynamic_index_in_dim(x, idx ^ d, 0, False)
        got.append(lax.ppermute(piece, AXES, swaps(n_lat, n_lon, masks[d])))
    if beside is not None:
        got, beside = lax.optimization_barrier((got, beside))
    total = lax.dynamic_index_in_dim(x, idx, 0, False).astype(F32)
    for g in got:
        total = total + g.astype(F32)
    return total.astype(BF16), beside


def packet_kernel(*refs):
    ins, out_ref = refs[:-1], refs[-1]
    size = ins[0].shape[0] - DKT
    total = ins[0][size:].astype(F32)
    for k, ref in enumerate(ins):
        out_ref[k * size : (k + 1) * size] = ref[:size]
        if k:
            total = total + ref[size:].astype(F32)
    out_ref[len(ins) * size :] = total.astype(BF16)


def gather_stage(packet, group, n_lat, n_lon, beside=None):
    masks = group_masks(group)
    got = [lax.ppermute(packet, AXES, swaps(n_lat, n_lon, masks[d])) for d in range(1, len(masks))]
    if beside is not None:
        got, beside = lax.optimization_barrier((got, beside))
    return [packet] + got, beside


def join(pieces):
    n, size = len(pieces), pieces[0].shape[0] - DKT
    return pl.pallas_call(
        packet_kernel,
        out_shape=jax.ShapeDtypeStruct((n * size + DKT, 16, 128), BF16),
        in_specs=[VM] * n,
        out_specs=VM,
        compiler_params=params(8),
        name="join",
        cost_estimate=cost(1),
    )(*pieces)


def body(field_in, sea_mask, mirror, kernel, norm_gain, proj_in, proj_out, cotangent):
    nrows, ncols, width = field_in.shape
    hidden = proj_in.shape[1]
    n_lat, n_lon = lax.axis_size("lat"), lax.axis_size("lon")
    assert ncols == COLS and nrows % 16 == 0 and n_lat % 2 == 0 and n_lon % 2 == 0
    lat, lon = lax.axis_index("lat"), lax.axis_index("lon")
    cells = nrows * ncols
    tt = nrows // SUB
    groups = stages(n_lat, n_lon)
    me = jnp.int32(0)
    for group in groups[1:]:
        me = (me << len(group)) + group_index(group, lat, lon)
    sc = jnp.stack(
        [1 - lon % 2, 1 - lat % 2, (lat == n_lat - 1).astype(jnp.int32), lon, lon * ncols, me, lat % 2, jnp.int32(0)]
    ).astype(jnp.int32)
    assert nrows == 128 and n_lon % 4 == 0
    hp = -(-hidden // HB) * HB
    win = jnp.pad(proj_in, ((0, CP - width), (0, hp - hidden)))
    wout = jnp.pad(proj_out.T, ((0, CP - width), (0, hp - hidden)))
    gain = jnp.pad(norm_gain, (0, CP - width)).reshape(1, CP)
    field_c = field_in.transpose(2, 1, 0)
    cot_c = cotangent.transpose(2, 1, 0)
    mask_c = sea_mask.T

    s = jax.ShapeDtypeStruct
    row_msg = s((3, COLS, CP), BF16)
    strip_msg = s((LT, 3 * tt * 8 + 32, 128), BF16)
    channels = pltpu.VMEM((CP * 8, 128), F32)
    cells_f32 = pltpu.VMEM((LT, cells, 128), F32)
    ext_f32 = pltpu.VMEM((LT, (tt + 6) * QC * 8, 128), F32)
    fold_f32 = pltpu.VMEM((LT, n_lon * 24, 128), F32)
    rows_f32 = pltpu.VMEM((6, COLS, CP), F32)
    taps_f32 = pltpu.VMEM((LT, 56, 128), F32)
    mf, p1, p2, q1, q2 = pl.pallas_call(
        prepare_kernel,
        out_shape=(s((LT, cells, 128), F32), row_msg, row_msg, strip_msg, strip_msg),
        in_specs=[SM, VM, VM],
        out_specs=(VM,) * 5,
        scratch_shapes=[channels, rows_f32],
        compiler_params=params(),
        name="prepare",
        cost_estimate=cost(3),
    )(sc, mask_c, field_c)
    bk = pl.pallas_call(
        back_kernel,
        out_shape=s((cells, CP), BF16),
        in_specs=[VM, VM],
        out_specs=VM,
        scratch_shapes=[channels, cells_f32],
        compiler_params=params(),
        name="back",
        cost_estimate=cost(3),
    )(mask_c, cot_c)

    lat1, lat2 = lat_swaps(n_lat, n_lon)
    lon1, lon2 = lon_swaps(n_lat, n_lon)

    def halo(q1, q2, p1, p2, beside):
        r1 = lax.ppermute(p1, AXES, lat1)
        r2 = lax.ppermute(p2, AXES, lat2)
        r1, r2, beside = lax.optimization_barrier((r1, r2, beside))
        q1, q2 = pl.pallas_call(
            corners_kernel,
            out_shape=(strip_msg, strip_msg),
            in_specs=[SM, VM, VM, ANY, ANY],
            out_specs=(ANY, ANY),
            scratch_shapes=[
                pltpu.VMEM((LT, 64, 128), F32),
                pltpu.VMEM((2, LT, 32, 128), BF16),
                pltpu.SemaphoreType.DMA((2,)),
            ],
            input_output_aliases={3: 0, 4: 1},
            compiler_params=params(4),
            name="corners",
            cost_estimate=cost(1),
        )(sc, r1, r2, q1, q2)
        s1 = lax.ppermute(q1, AXES, lon1)
        s2 = lax.ppermute(q2, AXES, lon2)
        return [s1, s2, r1, r2] + fold_gather(p2, r2, n_lat, n_lon), beside

    halos, bk = halo(q1, q2, p1, p2, bk)
    nf = len(halos) - 4
    count = 2 * (hp // 128) * (DWR // 16)
    devices = n_lat * n_lon
    per = -(-count // devices)
    half = per * devices // 2
    out, gc, g1, g2, q1, q2, dw, dgain = pl.pallas_call(
        lambda *refs: block_kernel(width, nf, *refs),
        out_shape=(
            s((width, COLS, nrows), BF16),
            s((LT, cells, 128), F32),
            row_msg,
            row_msg,
            strip_msg,
            strip_msg,
            s((per * devices, 16, 128), BF16),
            s((8, CP), F32),
        ),
        in_specs=[SM, SM] + [VM] * 4 + [ANY] * 4 + [VM] * len(halos),
        out_specs=(VM,) * 8,
        scratch_shapes=[
            taps_f32,
            fold_f32,
            ext_f32,
            pltpu.VMEM((cells, CP), F32),
            pltpu.VMEM((cells, CP), BF16),
            pltpu.VMEM((cells, hp), BF16),
            pltpu.VMEM((cells, hp), BF16),
            cells_f32,
            rows_f32,
            channels,
            pltpu.VMEM((CP, hp), BF16),
            pltpu.VMEM((CP, hp), BF16),
            pltpu.VMEM((width, COLS, nrows), BF16),
            pltpu.VMEM((cells, CP), BF16),
            pltpu.SemaphoreType.DMA((4,)),
        ],
        compiler_params=params(),
        name="block",
        cost_estimate=cost(18),
    )(sc, mirror, kernel, gain, mask_c, mf, win, wout, field_c, bk, *halos)

    first, _ = scatter_stage(dw, groups[0], lat, lon, n_lat, n_lon)
    ghalos, dgain = halo(q1, q2, g1, g2, dgain)
    gc_taps, dgain, _ = lax.optimization_barrier((gc, dgain, first))
    dk = pl.pallas_call(
        lambda *refs: taps_kernel(nf, *refs),
        out_shape=s((LT * DKR // 16, 16, 128), BF16),
        in_specs=[SM, SM] + [VM] * (len(halos) + 3),
        out_specs=VM,
        scratch_shapes=[fold_f32, ext_f32, pltpu.VMEM((LT, 49 * 8, 128), F32), pltpu.VMEM((LT, DKR, 128), F32)],
        compiler_params=params(),
        name="taps",
        cost_estimate=cost(1),
    )(sc, mirror, mf, gc_taps, dgain, *halos)
    x = first
    for k, group in enumerate(groups[1:]):
        beside = (dk, ghalos) if k == 0 else None
        x, beside = scatter_stage(x, group, lat, lon, n_lat, n_lon, beside)
        if beside is not None:
            dk, ghalos = beside
    grad_field = pl.pallas_call(
        lambda *refs: field_kernel(width, nf, *refs),
        out_shape=s((width, COLS, nrows), BF16),
        in_specs=[SM, SM] + [VM] * (len(ghalos) + 4),
        out_specs=VM,
        scratch_shapes=[taps_f32, fold_f32, ext_f32, pltpu.VMEM((LT, 3 * QC * 8, 128), F32), cells_f32, channels],
        compiler_params=params(),
        name="field",
        cost_estimate=cost(10),
    )(sc, mirror, kernel, mask_c, cot_c, gc, *ghalos)
    packet = jnp.concatenate([x, dk], axis=0)
    for group in reversed(groups[1:]):
        beside = grad_field if group is groups[1] else None
        pieces, beside = gather_stage(packet, group, n_lat, n_lon, beside)
        grad_field = grad_field if beside is None else beside
        packet = join(pieces)
    pieces, _ = gather_stage(packet, groups[0], n_lat, n_lon)
    factor = float(1.0 / np.sqrt(np.float32(nrows * n_lat * ncols * n_lon)))
    gin, gout, gk, gg = pl.pallas_call(
        lambda *refs: unpack_kernel(width, hidden, factor, per, half, *refs),
        out_shape=(s((width, hidden), F32), s((width, hidden), F32), s((49, width), F32), s((width,), F32)),
        in_specs=[SM, VM, VM],
        out_specs=(VM,) * 4,
        compiler_params=params(12),
        name="unpack",
        cost_estimate=cost(3),
    )(sc, pieces[0], pieces[1])
    return out.transpose(2, 1, 0), grad_field.transpose(2, 1, 0), gin, gout.T, gk, gg


def solution(mesh):
    in_specs = (
        P("lat", "lon", None),
        P("lat", "lon"),
        P(),
        P(),
        P(),
        P(),
        P(),
        P("lat", "lon", None),
    )
    out_specs = (P("lat", "lon", None), P("lat", "lon", None), P(), P(), P(), P())
    return jax.shard_map(body, mesh=mesh, in_specs=in_specs, out_specs=out_specs, check_vma=False)
```
